512 devices in a mesh: fsdp: 16 (over y, core), dp: 32 (over x, z).
Axes of the slice: x: 4, y: 8, z: 8, core: 2. Of those that a mesh axis runs over, the one named last changes fastest.
Arguments:
- tokens: bfloat16 [131072, 4096], P(('fsdp', 'dp')), may hold values from -6 to 6
- base_weight: bfloat16 [4096, 640], P('fsdp'), may hold values from -0.09375 to 0.09375
- cotangent: bfloat16 [131072, 640], P(('fsdp', 'dp')), may hold values from -0.29882812 to 0.29882812
- tenant_of_block: int32 [1024], replicated, may hold values from 0 to 95, as said below
- slot_of_tenant: int32 [96], replicated, may hold values from 0 to 95, as said below
- live_blocks: int32 [512], replicated, may hold values from 1 to 2, as said below
- down_param: float32 [96, 64, 4096], P('dp', 'fsdp'), may hold values from -0.09375 to 0.09375
- down_mom: float32 [96, 64, 4096], P('dp', 'fsdp'), may hold values from -6 to 6
- down_var: float32 [96, 64, 4096], P('dp', 'fsdp'), may hold values from 0.25 to 4
- up_param: float32 [96, 64, 640], P('dp', 'fsdp'), may hold values from -0.3 to 0.3
- up_mom: float32 [96, 64, 640], P('dp', 'fsdp'), may hold values from -6 to 6
- up_var: float32 [96, 64, 640], P('dp', 'fsdp'), may hold values from 0.25 to 4
Outputs:
- key_proj: bfloat16 [131072, 640], P(('fsdp', 'dp'))
- new_down: float32 [96, 64, 4096], P('dp', 'fsdp')
- new_down_mom: float32 [96, 64, 4096], P('dp', 'fsdp')
- new_down_var: float32 [96, 64, 4096], P('dp', 'fsdp')
- new_up: float32 [96, 64, 640], P('dp', 'fsdp')
- new_up_mom: float32 [96, 64, 640], P('dp', 'fsdp')
- new_up_var: float32 [96, 64, 640], P('dp', 'fsdp')
The draws below stay inside these ranges and needn't reach their ends.
Inputs may be any that keep to these rules, and one draw needn't show every extreme that they name: `tenant_of_block`: slot s lives on dp index s // 3. For every dp index d and owner dp index e, the blocks of all devices at dp index d (device index = fsdp index * 32 + dp index) name at most 2 different tenants whose slots lie on e, and some pair reaches 2. `slot_of_tenant`: A permutation of the tenants. Device i (index = fsdp index * 32 + dp index) holds live blocks in its first live_blocks[i] places; device 0 is full.
All inputs are finite; a program needn't handle non-finite values.
Results may differ from the reference program's by a relative error of at most 0.0052.
Values may be sent and summed in bfloat16 or wider, within the bound.
A program may use at most 64 MiB of HBM per device.

```python
import math
import jax
import jax.numpy as jnp
from jax import lax

D = 4096
KV = 640
R = 64
BLOCK = 128
SLOTS = 2
SEG_CAP = 2
TEN_DEV = 3
TENANTS = 96
SEGS = 1024
TOKENS = 131072
N_FSDP = 16
N_DP = 32


def routing_tables(key):
    base_key = jax.random.fold_in(key, 7)
    key_perm, key_offset, key_owner, key_rank, key_count = jax.random.split(base_key, 5)
    groups = TENANTS // TEN_DEV
    places = jnp.arange(SEGS, dtype=jnp.int32)
    slot_of = jax.random.permutation(key_perm, TENANTS).astype(jnp.int32)
    inverse = jnp.zeros((TENANTS,), jnp.int32).at[slot_of].set(jnp.arange(TENANTS, dtype=jnp.int32))
    offsets = jax.random.randint(key_offset, (groups, groups), 0, TEN_DEV, dtype=jnp.int32)
    owner_pick = jax.random.randint(key_owner, (SEGS,), 0, groups, dtype=jnp.int32)
    rank_pick = jax.random.randint(key_rank, (SEGS,), 0, SLOTS, dtype=jnp.int32)
    owner_pick = jnp.where(places < 2, 0, owner_pick)
    rank_pick = jnp.where(places < 2, places, rank_pick)
    group_of = places // SEG_CAP % groups
    local_pick = (offsets[group_of, owner_pick] + rank_pick) % TEN_DEV
    slot_pick = owner_pick * TEN_DEV + local_pick
    tenant_ids = inverse[slot_pick]
    live_count = jax.random.randint(key_count, (SEGS // SEG_CAP,), 1, SEG_CAP + 1, dtype=jnp.int32)
    live_count = live_count.at[0].set(SEG_CAP)
    return (tenant_ids, slot_of, live_count)


def draw_tenant_of_block(key, part):
    return routing_tables(key)[0]


def draw_slot_of_tenant(key, part):
    return routing_tables(key)[1]


def draw_live_blocks(key, part):
    return routing_tables(key)[2]


def level_of(stream_key, shape, cuts, smallest, largest):
    def one(position, shards_of):
        heights = jax.random.uniform(jax.random.fold_in(jax.random.fold_in(stream_key, 6), position), (shards_of,), jnp.float32, smallest / len(cuts), largest / len(cuts))
        return jnp.repeat(jnp.exp(heights), shape[position] // shards_of).reshape((-1,) + (1,) * (len(shape) - position - 1))

    gain = one(*cuts[0])
    for cut in cuts[1:]:
        gain = gain * one(*cut)
    return gain


def noise(own_key, dims, spread, most, cuts=(), kind=jnp.bfloat16):
    values = jax.random.normal(own_key, dims, jnp.float32) * spread
    if len(cuts) > 0:
        values = level_of(own_key, dims, cuts, -0.22, 0.18) * values
    return jnp.clip(values, min=-most, max=most).astype(kind)


def setup_inputs(seed: int = 0) -> dict:
    key_of = jax.random.split(jax.random.key(seed), 13)
    return {
        "tokens": noise(key_of[0], (TOKENS, D), 1.0, 6.0, ((0, 512),)),
        "base_weight": noise(key_of[1], (D, KV), D ** -0.5, 0.09375, ((0, 16),)),
        "cotangent": noise(key_of[2], (TOKENS, KV), 0.05, 0.29882812, ((0, 512),)),
        "tenant_of_block": draw_tenant_of_block(jax.random.fold_in(key_of[12], 71), 0),
        "slot_of_tenant": draw_slot_of_tenant(jax.random.fold_in(key_of[12], 71), 0),
        "live_blocks": draw_live_blocks(jax.random.fold_in(key_of[12], 71), 0),
        "down_param": noise(key_of[6], (TENANTS, R, D), D ** -0.5, 0.09375, ((0, 32), (1, 16)), jnp.float32),
        "down_mom": noise(key_of[7], (TENANTS, R, D), 1.0, 6.0, ((0, 32), (1, 16)), jnp.float32),
        "down_var": jnp.clip(jnp.exp(math.log(4.0) - 2.7725887 * jax.random.uniform(key_of[8], (TENANTS, R, D), jnp.float32) ** level_of(key_of[8], (TENANTS, R, D), ((0, 32), (1, 16)), -0.2, 0.2)), 0.25, 4.0),
        "up_param": noise(key_of[9], (TENANTS, R, KV), 0.05, 0.3, ((0, 32), (1, 16)), jnp.float32),
        "up_mom": noise(key_of[10], (TENANTS, R, KV), 1.0, 6.0, ((0, 32), (1, 16)), jnp.float32),
        "up_var": jnp.clip(jnp.exp(math.log(4.0) - 2.7725887 * jax.random.uniform(key_of[11], (TENANTS, R, KV), jnp.float32) ** level_of(key_of[11], (TENANTS, R, KV), ((0, 32), (1, 16)), -0.2, 0.2)), 0.25, 4.0),
    }


adapter_scale = 2.0
learn_rate = 0.01
beta_one = 0.9
beta_two = 0.99
adam_eps = 1e-08
correct_one = 1.0 - 0.9 ** 8
correct_two = 1.0 - 0.99 ** 8

def adam_update(master, moment, second, gradient):
    moment_new = beta_one * moment + (1.0 - beta_one) * gradient
    second_new = beta_two * second + (1.0 - beta_two) * gradient * gradient
    master_new = master - learn_rate * (moment_new / correct_one) / (jnp.sqrt(second_new / correct_two) + adam_eps)
    return (master_new, moment_new, second_new)

def by_group(array):
    shaped = array.reshape((N_FSDP, N_DP, SEG_CAP) + array.shape[1:])
    moved = jnp.swapaxes(shaped, 0, 1)
    return moved.reshape((N_DP, N_FSDP * SEG_CAP) + array.shape[1:])

def reference(tokens, base_weight, cotangent, tenant_of_block, slot_of_tenant, live_blocks, down_param, down_mom, down_var, up_param, up_mom, up_var):
    seg_total = tenant_of_block.shape[0]
    block_slot = slot_of_tenant[tenant_of_block].astype(jnp.int32)
    places = jnp.arange(seg_total, dtype=jnp.int32)
    device = places // SEG_CAP
    is_live = places % SEG_CAP < live_blocks[device]
    down_used = down_param.astype(jnp.bfloat16)
    up_used = up_param.astype(jnp.bfloat16)
    block_rows = by_group(tokens.reshape(seg_total, BLOCK, D))
    block_cot = by_group(cotangent.reshape(seg_total, BLOCK, KV))
    group_slot = by_group(block_slot)
    group_live = by_group(is_live)

    def block_step(state_sum, block_item):
        acc_down, acc_up = state_sum
        rows_in, cot_in, slot_id, block_is_active = block_item
        down_rows = down_used[slot_id]
        up_row_values = up_used[slot_id]
        frozen_output = jnp.dot(rows_in, base_weight, preferred_element_type=jnp.float32)
        hidden_state = jnp.dot(rows_in, down_rows.T, preferred_element_type=jnp.float32).astype(jnp.bfloat16)
        adapter_output = jnp.dot(hidden_state, up_row_values, preferred_element_type=jnp.float32)
        key_row_values = jnp.where(block_is_active, frozen_output + adapter_scale * adapter_output, jnp.float32(0.0)).astype(jnp.bfloat16)
        cotangent_active = jnp.where(block_is_active, cot_in, jnp.zeros_like(cot_in))
        up_gradient = (adapter_scale * jnp.dot(hidden_state.T, cotangent_active, preferred_element_type=jnp.float32)).astype(jnp.bfloat16)
        hidden_gradient = (adapter_scale * jnp.dot(cotangent_active, up_row_values.T, preferred_element_type=jnp.float32)).astype(jnp.bfloat16)
        grad_down = jnp.dot(hidden_gradient.T, rows_in, preferred_element_type=jnp.float32).astype(jnp.bfloat16)
        acc_down = acc_down.at[slot_id].add(grad_down.astype(jnp.float32))
        acc_up = acc_up.at[slot_id].add(up_gradient.astype(jnp.float32))
        return ((acc_down, acc_up), key_row_values)

    def group_step(total_sum, group_item):
        total_down, total_up = total_sum
        start_part = (jnp.zeros(down_param.shape, jnp.float32), jnp.zeros(up_param.shape, jnp.float32))
        (part_down, part_up), key_group = lax.scan(block_step, start_part, group_item)
        part_down = lax.optimization_barrier(part_down.astype(jnp.bfloat16)).astype(jnp.float32)
        part_up = lax.optimization_barrier(part_up.astype(jnp.bfloat16)).astype(jnp.float32)
        return ((total_down + part_down, total_up + part_up), key_group)
    start_sum = (jnp.zeros(down_param.shape, jnp.float32), jnp.zeros(up_param.shape, jnp.float32))
    (sum_down, sum_up), key_groups = lax.scan(group_step, start_sum, (block_rows, block_cot, group_slot, group_live))
    key_back = jnp.swapaxes(key_groups.reshape(N_DP, N_FSDP, SEG_CAP, BLOCK, KV), 0, 1)
    key_proj = key_back.reshape(seg_total * BLOCK, KV)
    new_down, new_down_mom, new_down_var = adam_update(down_param, down_mom, down_var, sum_down)
    new_up, new_up_mom, new_up_var = adam_update(up_param, up_mom, up_var, sum_up)
    return (key_proj, new_down, new_down_mom, new_down_var, new_up, new_up_mom, new_up_var)
```

```python
import functools

import jax
import jax.numpy as jnp
from jax import lax
from jax.experimental import pallas as pl
from jax.experimental.pallas import tpu as pltpu
from jax.sharding import PartitionSpec as P

SLOTS = 2
LANES = 128
NX, NZ = 4, 8
GATHER_CHUNKS = ((80, "zx"), (80, "xz"))
SCATTER_CHUNKS = ((64, "xz"), (64, "xz"), (32, "zx"))
PIECE = 160
VMEM_LIMIT = 60 * 1024 * 1024


adapter_scale = 2.0
learn_rate = 0.01
beta_one = 0.9
beta_two = 0.99
adam_eps = 1e-08
correct_one = 1.0 - 0.9**8
correct_two = 1.0 - 0.99**8


def adam_update(master, moment, second, gradient):
    moment_new = beta_one * moment + (1.0 - beta_one) * gradient
    second_new = beta_two * second + (1.0 - beta_two) * gradient * gradient
    master_new = master - learn_rate * (moment_new / correct_one) / (
        jnp.sqrt(second_new / correct_two) + adam_eps
    )
    return (master_new, moment_new, second_new)


def dp_at(x, z):
    return x * NZ + z


def ring(send, n, me, unit, row_of):
    half = (unit + 1) // 2
    for step in range(1, n // 2 + 1):
        last = step == n // 2
        lo = (0, half if last else unit)
        hi = (half if last else 0, unit)
        out_r = row_of(lax.rem(me - (step - 1) + n, n))
        out_l = row_of(lax.rem(me + (step - 1), n))
        in_r = row_of(lax.rem(me - step + n, n))
        in_l = row_of(lax.rem(me + step, n))
        wait_r = send(+1, out_r + lo[0], lo[1] - lo[0], in_r + lo[0])
        wait_l = send(-1, out_l + hi[0], hi[1] - hi[0], in_l + hi[0])
        yield
        wait_r()
        wait_l()


def gather_kernel(own, slot_ref, *refs):
    count = len(GATHER_CHUNKS)
    shards, outs = refs[:count], refs[count : 2 * count]
    tables, sends = refs[2 * count : 3 * count], refs[3 * count : 4 * count]
    send_sem, recv_sem, fs_send, fs_recv = refs[4 * count :]
    members = lax.axis_size("fsdp")
    blocks = sends[0].shape[0]
    cap = blocks // members
    member = lax.axis_index("fsdp")
    group = lax.axis_index("dp")
    x, z = group // NZ, lax.rem(group, NZ)

    def shifted(axis, delta):
        if axis == "x":
            return dp_at(lax.rem(x + delta + NX, NX), z)
        return dp_at(x, lax.rem(z + delta + NZ, NZ))

    barrier = pltpu.get_barrier_semaphore()
    for axis in ("x", "z"):
        for delta in (1, -1):
            pl.semaphore_signal(
                barrier, inc=1, device_id={"dp": shifted(axis, delta)},
                device_id_type=pl.DeviceIdType.MESH,
            )
    for off in range(1, members):
        pl.semaphore_signal(
            barrier, inc=1, device_id={"fsdp": lax.rem(member + off, members)},
            device_id_type=pl.DeviceIdType.MESH,
        )
    for c, (_, order) in enumerate(GATHER_CHUNKS):
        minor_n = NZ if order == "zx" else NX
        major, minor = (x, z) if order == "zx" else (z, x)
        tables[c][pl.ds((major * minor_n + minor) * own, own)] = shards[c][...]
    pl.semaphore_wait(barrier, 4 + members - 1)

    pending = []
    used = [0]

    def mover(table, axis):
        def send(delta, row, size, row_in):
            k = used[0]
            used[0] += 1
            dst = {"dp": shifted(axis, delta)}
            out = pltpu.make_async_remote_copy(
                src_ref=table.at[pl.ds(row, size)], dst_ref=table.at[pl.ds(row, size)],
                send_sem=send_sem.at[k], recv_sem=recv_sem.at[k],
                device_id=dst, device_id_type=pl.DeviceIdType.MESH,
            )
            out.start()
            pending.append(out)
            landed = pltpu.make_async_remote_copy(
                src_ref=table.at[pl.ds(row_in, size)], dst_ref=table.at[pl.ds(row_in, size)],
                send_sem=send_sem.at[k], recv_sem=recv_sem.at[k],
                device_id=dst, device_id_type=pl.DeviceIdType.MESH,
            )
            return landed.wait_recv

        return send

    def chunk_flow(c, order):
        table = tables[c]
        first, second = order
        n1, n2 = (NZ, NX) if order == "zx" else (NX, NZ)
        minor, major = (z, x) if order == "zx" else (x, z)
        yield from ring(
            mover(table, first), n1, minor, own, lambda i: (major * n1 + i) * own
        )
        yield from ring(mover(table, second), n2, major, n1 * own, lambda i: i * n1 * own)

        def pick(b, carry):
            sends[c][pl.ds(b, 1)] = table[pl.ds(slot_ref[c * blocks + b], 1)]
            return carry

        lax.fori_loop(0, blocks, pick, 0)
        outs[c][pl.ds(member * cap, cap)] = sends[c][pl.ds(member * cap, cap)]
        for off in range(1, members):
            peer = lax.rem(member + off, members)
            k = c * members + off
            out = pltpu.make_async_remote_copy(
                src_ref=sends[c].at[pl.ds(peer * cap, cap)],
                dst_ref=outs[c].at[pl.ds(member * cap, cap)],
                send_sem=fs_send.at[k], recv_sem=fs_recv.at[k],
                device_id={"fsdp": peer}, device_id_type=pl.DeviceIdType.MESH,
            )
            out.start()
            pending.append(out)

    flows = [chunk_flow(c, order) for c, (_, order) in enumerate(GATHER_CHUNKS)]
    while flows:
        alive = []
        for flow in flows:
            try:
                next(flow)
                alive.append(flow)
            except StopIteration:
                pass
        flows = alive
    for c in range(count):
        for off in range(1, members):
            source = lax.rem(member - off + members, members)
            k = c * members + off
            pltpu.make_async_remote_copy(
                src_ref=sends[c].at[pl.ds(source * cap, cap)],
                dst_ref=outs[c].at[pl.ds(source * cap, cap)],
                send_sem=fs_send.at[k], recv_sem=fs_recv.at[k],
                device_id={"fsdp": source}, device_id_type=pl.DeviceIdType.MESH,
            ).wait_recv()
    for copy in pending:
        copy.wait_send()


def gather_adapters(packed, slot_tab, members, cap):
    own = packed.shape[0]
    tenants = own * NX * NZ
    count = len(GATHER_CHUNKS)
    blocks = members * cap
    shards, start = [], 0
    for rows, _ in GATHER_CHUNKS:
        shards.append(packed[:, start : start + rows])
        start += rows
    vmem = pl.BlockSpec(memory_space=pltpu.VMEM)
    moves = count * 2 * (NX // 2 + NZ // 2)
    return pl.pallas_call(
        functools.partial(gather_kernel, own),
        out_shape=[
            jax.ShapeDtypeStruct((blocks, rows, LANES), jnp.bfloat16) for rows, _ in GATHER_CHUNKS
        ],
        in_specs=[pl.BlockSpec(memory_space=pltpu.SMEM)] + [vmem] * count,
        out_specs=[vmem] * count,
        scratch_shapes=[pltpu.VMEM((tenants, rows, LANES), jnp.bfloat16) for rows, _ in GATHER_CHUNKS]
        + [pltpu.VMEM((blocks, rows, LANES), jnp.bfloat16) for rows, _ in GATHER_CHUNKS]
        + [
            pltpu.SemaphoreType.DMA((moves,)),
            pltpu.SemaphoreType.DMA((moves,)),
            pltpu.SemaphoreType.DMA((count * members,)),
            pltpu.SemaphoreType.DMA((count * members,)),
        ],
        compiler_params=pltpu.CompilerParams(
            collective_id=0, has_side_effects=True, vmem_limit_bytes=VMEM_LIMIT
        ),
        name="gather_adapters",
    )(slot_tab, *shards)


def scatter_kernel(own, tab, *refs):
    count = len(SCATTER_CHUNKS)
    take = lambda i: refs[i * count : (i + 1) * count]
    grads, outs, lands, runs, sends1, lands1, sends2, lands2 = (take(i) for i in range(8))
    fs_send, fs_recv, s1_send, s1_recv, s2_send, s2_recv = refs[8 * count :]
    members = lax.axis_size("fsdp")
    blocks = grads[0].shape[0]
    cap = blocks // members
    pairs = NX * NZ * SLOTS
    sums = NX * NZ * own
    member = lax.axis_index("fsdp")
    group = lax.axis_index("dp")
    x, z = group // NZ, lax.rem(group, NZ)
    mesh_ids = pl.DeviceIdType.MESH
    at_x = lambda i: {"dp": dp_at(i, z)}
    at_z = lambda i: {"dp": dp_at(x, i)}

    barrier = pltpu.get_barrier_semaphore()
    for off in range(1, members):
        pl.semaphore_signal(
            barrier, inc=1, device_id={"fsdp": lax.rem(member + off, members)},
            device_id_type=mesh_ids,
        )
    for off in range(1, NX):
        pl.semaphore_signal(
            barrier, inc=1, device_id=at_x(lax.rem(x + off, NX)), device_id_type=mesh_ids
        )
    for off in range(1, NZ):
        pl.semaphore_signal(
            barrier, inc=1, device_id=at_z(lax.rem(z + off, NZ)), device_id_type=mesh_ids
        )
    pl.semaphore_wait(barrier, members - 1 + NX - 1 + NZ - 1)

    pending = []

    def exchange(src, dst, n, me, rows, target, send_sem, recv_sem, base):
        waits = []
        for off in range(1, n):
            peer = lax.rem(me + off, n)
            source = lax.rem(me - off + n, n)
            copy = pltpu.make_async_remote_copy(
                src_ref=src.at[pl.ds(peer * rows, rows)], dst_ref=dst.at[pl.ds(me * rows, rows)],
                send_sem=send_sem.at[base + off], recv_sem=recv_sem.at[base + off],
                device_id=target(peer), device_id_type=mesh_ids,
            )
            copy.start()
            pending.append(copy)
            waits.append(
                pltpu.make_async_remote_copy(
                    src_ref=src.at[pl.ds(source * rows, rows)],
                    dst_ref=dst.at[pl.ds(source * rows, rows)],
                    send_sem=send_sem.at[base + off], recv_sem=recv_sem.at[base + off],
                    device_id=target(source), device_id_type=mesh_ids,
                ).wait_recv
            )
        dst[pl.ds(me * rows, rows)] = src[pl.ds(me * rows, rows)]
        return waits

    fs_waits = [
        exchange(
            grads[c], lands[c], members, member, cap, lambda i: {"fsdp": i}, fs_send, fs_recv,
            c * members,
        )
        for c in range(count)
    ]
    waits1 = []
    for c, (_, order) in enumerate(SCATTER_CHUNKS):
        n1, first = (NX, x) if order[0] == "x" else (NZ, z)
        target = at_x if order[0] == "x" else at_z
        kind = blocks + (0 if order[0] == "x" else pairs)
        run, send, land1 = runs[c], sends1[c], lands1[c]
        run[pl.ds(blocks, 1)] = jnp.zeros((1,) + run.shape[1:], run.dtype)
        land1[pl.ds(pairs, 1)] = jnp.zeros((1,) + land1.shape[1:], land1.dtype)
        for wait in fs_waits[c]:
            wait()

        def add(b, carry, run=run, land=lands[c]):
            run[pl.ds(b, 1)] = land[pl.ds(b, 1)].astype(jnp.float32) + run[pl.ds(tab[b], 1)]
            return carry

        lax.fori_loop(0, blocks, add, 0)

        def pick(p, carry, run=run, send=send, kind=kind):
            send[pl.ds(p, 1)] = run[pl.ds(tab[kind + p], 1)].astype(jnp.bfloat16)
            return carry

        lax.fori_loop(0, pairs, pick, 0)
        waits1.append(
            exchange(send, land1, n1, first, pairs // n1, target, s1_send, s1_recv, c * NZ)
        )
    waits2 = []
    for c, (_, order) in enumerate(SCATTER_CHUNKS):
        n1, n2, second = (NX, NZ, z) if order[0] == "x" else (NZ, NX, x)
        target = at_z if order[0] == "x" else at_x
        kind = blocks + 2 * pairs + (0 if order[0] == "x" else sums)
        for wait in waits1[c]:
            wait()

        def total(q, carry, n1=n1, n2=n2, kind=kind, land1=lands1[c], send2=sends2[c]):
            acc = land1[pl.ds(tab[kind + q], 1)].astype(jnp.float32)
            for f in range(1, n1):
                acc = acc + land1[pl.ds(tab[kind + f * (n2 * own) + q], 1)].astype(jnp.float32)
            send2[pl.ds(q, 1)] = acc.astype(jnp.bfloat16)
            return carry

        lax.fori_loop(0, n2 * own, total, 0)
        waits2.append(
            exchange(sends2[c], lands2[c], n2, second, own, target, s2_send, s2_recv, c * NZ)
        )
    for c, (_, order) in enumerate(SCATTER_CHUNKS):
        n2 = NZ if order[0] == "x" else NX
        for wait in waits2[c]:
            wait()
        for j in range(own):
            acc = lands2[c][j].astype(jnp.float32)
            for s in range(1, n2):
                acc = acc + lands2[c][s * own + j].astype(jnp.float32)
            outs[c][j] = acc
    for copy in pending:
        copy.wait_send()


def scatter_gradients(packed, tab, own, members):
    count = len(SCATTER_CHUNKS)
    blocks = packed.shape[0]
    pairs = NX * NZ * SLOTS
    grads, start = [], 0
    for rows, _ in SCATTER_CHUNKS:
        grads.append(packed[:, start : start + rows])
        start += rows
    vmem = pl.BlockSpec(memory_space=pltpu.VMEM)
    bf, f32 = jnp.bfloat16, jnp.float32
    second = [(NZ if order[0] == "x" else NX) * own for _, order in SCATTER_CHUNKS]
    buffers = lambda sizes, kind: [
        pltpu.VMEM((size, rows, LANES), kind) for size, (rows, _) in zip(sizes, SCATTER_CHUNKS)
    ]
    outs = pl.pallas_call(
        functools.partial(scatter_kernel, own),
        out_shape=[jax.ShapeDtypeStruct((own, rows, LANES), f32) for rows, _ in SCATTER_CHUNKS],
        in_specs=[pl.BlockSpec(memory_space=pltpu.SMEM)] + [vmem] * count,
        out_specs=[vmem] * count,
        scratch_shapes=buffers([blocks] * count, bf)
        + buffers([blocks + 1] * count, f32)
        + buffers([pairs] * count, bf)
        + buffers([pairs + 1] * count, bf)
        + buffers(second, bf)
        + buffers(second, bf)
        + [pltpu.SemaphoreType.DMA((count * members,))] * 2
        + [pltpu.SemaphoreType.DMA((count * NZ,))] * 4,
        compiler_params=pltpu.CompilerParams(
            collective_id=1, has_side_effects=True, vmem_limit_bytes=VMEM_LIMIT
        ),
        name="scatter_gradients",
    )(tab, *grads)
    return jnp.concatenate(outs, axis=1)


def lane_rows(array):
    lead, (rows, width) = array.shape[:-2], array.shape[-2:]
    parts = array.reshape(lead + (rows, width // LANES, LANES))
    return jnp.swapaxes(parts, -3, -2).reshape(lead + (rows * width // LANES, LANES))


def from_lane_rows(array, rows):
    lead, count = array.shape[:-2], array.shape[-2] // rows
    parts = array.reshape(lead + (count, rows, LANES))
    return jnp.swapaxes(parts, -3, -2).reshape(lead + (rows, count * LANES))


def pack(down, up):
    parts = jnp.concatenate([lane_rows(down), lane_rows(up)], axis=-2)
    room = PIECE - parts.shape[-2]
    return jnp.pad(parts, [(0, 0)] * (parts.ndim - 2) + [(0, room), (0, 0)])


def local(
    tokens,
    base_weight,
    cotangent,
    tenant_of_block,
    slot_of_tenant,
    live_blocks,
    down_param,
    down_mom,
    down_var,
    up_param,
    up_mom,
    up_var,
):
    groups = lax.axis_size("dp")
    members = lax.axis_size("fsdp")
    own_count = down_param.shape[0]
    tenants = own_count * groups
    seg_total = tenant_of_block.shape[0]
    segment_capacity = seg_total // (groups * members)
    block_row_count = tokens.shape[0] // segment_capacity
    feat_width = tokens.shape[1]
    heads_weight = base_weight.shape[1]
    rank_sh = down_param.shape[1]
    me_group = lax.axis_index("dp")
    me_member = lax.axis_index("fsdp")
    highest = lax.Precision.HIGHEST
    tenant_range = jnp.arange(tenants, dtype=jnp.int32)
    block_slot = jnp.sum(
        jnp.where(tenant_of_block[:, None] == tenant_range[None, :], slot_of_tenant[None, :], 0),
        axis=1,
    )
    block_group = jnp.arange(seg_total, dtype=jnp.int32) // segment_capacity % groups
    slot_onehot = (block_slot[:, None] == tenant_range[None, :]).astype(jnp.float32)
    group_onehot = (block_group[:, None] == jnp.arange(groups, dtype=jnp.int32)[None, :]).astype(
        jnp.float32
    )
    need_count = jnp.dot(group_onehot.T, slot_onehot, precision=highest)
    need_int = (need_count > 0.5).astype(jnp.int32).reshape(groups, groups, own_count)
    rank_tab = jnp.cumsum(need_int, axis=2) - need_int
    rank_rows = jnp.dot(
        group_onehot, rank_tab.reshape(groups, tenants).astype(jnp.float32), precision=highest
    )
    block_rank = jnp.sum(rank_rows * slot_onehot, axis=1).astype(jnp.int32)
    block_pos = block_slot // own_count * SLOTS + block_rank
    group_blocks = (
        jnp.arange(members, dtype=jnp.int32)[:, None] * groups + me_group
    ) * segment_capacity + jnp.arange(segment_capacity, dtype=jnp.int32)[None, :]
    pick_pos = jnp.take(block_pos, group_blocks, axis=0).reshape(-1)
    table_pick = jnp.take(block_slot, group_blocks, axis=0).reshape(-1)
    pick_xz = table_pick
    owner = table_pick // own_count
    pick_zx = (owner % NZ * NX + owner // NZ) * own_count + table_pick % own_count
    slot_tab = jnp.concatenate(
        [pick_xz if order == "zx" else pick_zx for _, order in GATHER_CHUNKS]
    )
    down_used = down_param.astype(jnp.bfloat16)
    up_used = up_param.astype(jnp.bfloat16)
    pieces = gather_adapters(pack(down_used, up_used), slot_tab, members, segment_capacity)
    pieces = jnp.concatenate(pieces, axis=1)
    down_rows = rank_sh * feat_width // LANES
    up_rows = rank_sh * heads_weight // LANES
    by_rank = lambda rows: jnp.swapaxes(
        from_lane_rows(rows, rank_sh).reshape(members, segment_capacity, rank_sh, -1), 0, 1
    ).reshape(segment_capacity, members * rank_sh, -1)
    block_down = by_rank(pieces[:, :down_rows])
    block_up = by_rank(pieces[:, down_rows : down_rows + up_rows])
    own_blocks = members * segment_capacity
    place = jnp.arange(own_blocks, dtype=jnp.int32)
    same = (pick_pos[:, None] == pick_pos[None, :]) & (place[None, :] < place[:, None])
    earlier = jnp.max(jnp.where(same, place[None, :], -1), axis=1)
    earlier = jnp.where(earlier < 0, own_blocks, earlier)
    pair_range = jnp.arange(groups * SLOTS, dtype=jnp.int32)
    final = jnp.max(jnp.where(pick_pos[None, :] == pair_range[:, None], place[None, :], -1), axis=1)
    final = jnp.where(final < 0, own_blocks, final)
    final_zx = jnp.swapaxes(final.reshape(NX, NZ, SLOTS), 0, 1).reshape(-1)
    rank_or = jnp.where(need_int == 1, rank_tab, -1).reshape(NX, NZ, NX, NZ, own_count)
    me_x, me_z = me_group // NZ, me_group % NZ
    to_x = jnp.take(jnp.take(rank_or, me_z, axis=1), me_x, axis=1)
    to_z = jnp.take(jnp.take(rank_or, me_x, axis=0), me_z, axis=2)

    def landed(ranks):
        first, second, _ = ranks.shape
        base = jnp.arange(first * second, dtype=jnp.int32).reshape(first, second, 1) * SLOTS
        return jnp.where(ranks >= 0, base + ranks, groups * SLOTS).reshape(-1)

    sum_tab = jnp.concatenate([earlier, final, final_zx, landed(to_x), landed(to_z)])
    frozen_output = jnp.dot(
        tokens,
        lax.all_gather(base_weight, "fsdp", axis=0, tiled=True),
        preferred_element_type=jnp.float32,
    )
    my_device = me_member * groups + me_group
    live_count = live_blocks[my_device]
    live_mask = (jnp.arange(segment_capacity, dtype=jnp.int32) < live_count)[:, None, None]
    blocks = tokens.reshape(segment_capacity, block_row_count, feat_width)
    hidden_state = jnp.einsum(
        "cbx,crx->cbr", blocks, block_down, preferred_element_type=jnp.float32
    ).astype(jnp.bfloat16)
    adapter_output = jnp.einsum(
        "cbr,crk->cbk", hidden_state, block_up, preferred_element_type=jnp.float32
    )
    key_blocks = jnp.where(
        live_mask,
        frozen_output.reshape(segment_capacity, block_row_count, heads_weight)
        + adapter_scale * adapter_output,
        jnp.float32(0.0),
    )
    key_proj = key_blocks.astype(jnp.bfloat16).reshape(tokens.shape[0], heads_weight)
    cot_blocks = cotangent.reshape(segment_capacity, block_row_count, heads_weight)
    cotangent_active = jnp.where(live_mask, cot_blocks, jnp.zeros_like(cot_blocks))
    up_gradient = (
        adapter_scale
        * jnp.einsum(
            "cbr,cbk->crk", hidden_state, cotangent_active, preferred_element_type=jnp.float32
        )
    ).astype(jnp.bfloat16)
    hidden_gradient = (
        adapter_scale
        * jnp.einsum("cbk,crk->cbr", cotangent_active, block_up, preferred_element_type=jnp.float32)
    ).astype(jnp.bfloat16)
    grad_down = jnp.einsum(
        "cbr,cbx->crx", hidden_gradient, blocks, preferred_element_type=jnp.float32
    ).astype(jnp.bfloat16)
    by_member = lambda rows: jnp.swapaxes(
        rows.reshape(segment_capacity, members, rank_sh, -1), 0, 1
    ).reshape(own_blocks, rank_sh, -1)
    grad_rows = pack(by_member(grad_down), by_member(up_gradient))
    sum_rows = scatter_gradients(grad_rows, sum_tab, own_count, members)
    sum_down = from_lane_rows(sum_rows[:, :down_rows], rank_sh)
    sum_up = from_lane_rows(sum_rows[:, down_rows : down_rows + up_rows], rank_sh)
    new_down, new_down_mom, new_down_var = adam_update(down_param, down_mom, down_var, sum_down)
    new_up, new_up_mom, new_up_var = adam_update(up_param, up_mom, up_var, sum_up)
    return (key_proj, new_down, new_down_mom, new_down_var, new_up, new_up_mom, new_up_var)


def solution(mesh):
    return jax.shard_map(
        local,
        mesh=mesh,
        in_specs=(
            P(("fsdp", "dp"), None),
            P("fsdp", None),
            P(("fsdp", "dp"), None),
            P(),
            P(),
            P(),
            P("dp", "fsdp", None),
            P("dp", "fsdp", None),
            P("dp", "fsdp", None),
            P("dp", "fsdp", None),
            P("dp", "fsdp", None),
            P("dp", "fsdp", None),
        ),
        out_specs=(
            P(("fsdp", "dp"), None),
            P("dp", "fsdp", None),
            P("dp", "fsdp", None),
            P("dp", "fsdp", None),
            P("dp", "fsdp", None),
            P("dp", "fsdp", None),
            P("dp", "fsdp", None),
        ),
        check_vma=False,
    )
```

```python
import functools

import jax
import jax.numpy as jnp
from jax import lax
from jax.experimental import pallas as pl
from jax.experimental.pallas import tpu as pltpu
from jax.sharding import PartitionSpec as P

SLOTS = 2
LANES = 128
NX, NZ = 4, 8
GATHER_CHUNKS = ((80, "zx"), (80, "xz"))
SCATTER_CHUNKS = ((32, "zx"), (48, "xz"), (48, "xz"), (32, "xz"))
FLOW_ORDER = (0, 1, 0, 1, 2, 0, 0, 1, 2, 1, 0, 1, 2, 1, 0, 2)
PIECE = 160
VMEM_LIMIT = 60 * 1024 * 1024


adapter_scale = 2.0
learn_rate = 0.01
beta_one = 0.9
beta_two = 0.99
adam_eps = 1e-08
correct_one = 1.0 - 0.9**8
correct_two = 1.0 - 0.99**8


def adam_update(master, moment, second, gradient):
    moment_new = beta_one * moment + (1.0 - beta_one) * gradient
    second_new = beta_two * second + (1.0 - beta_two) * gradient * gradient
    master_new = master - learn_rate * (moment_new / correct_one) / (
        jnp.sqrt(second_new / correct_two) + adam_eps
    )
    return (master_new, moment_new, second_new)


def dp_at(x, z):
    return x * NZ + z


def ring(send, n, me, unit, row_of, arrived=None):
    half = (unit + 1) // 2
    for step in range(1, n // 2 + 1):
        last = step == n // 2
        lo = (0, half if last else unit)
        hi = (half if last else 0, unit)
        out_r = row_of(lax.rem(me - (step - 1) + n, n))
        out_l = row_of(lax.rem(me + (step - 1), n))
        in_r = row_of(lax.rem(me - step + n, n))
        in_l = row_of(lax.rem(me + step, n))
        wait_r = send(+1, out_r + lo[0], lo[1] - lo[0], in_r + lo[0])
        wait_l = send(-1, out_l + hi[0], hi[1] - hi[0], in_l + hi[0])
        yield
        wait_r()
        wait_l()
        if arrived is not None:
            arrived(lax.rem(me - step + n, n), *lo)
            arrived(lax.rem(me + step, n), *hi)


def gather_kernel(own, slot_ref, *refs):
    count = len(GATHER_CHUNKS)
    shards, outs = refs[:count], refs[count + 1 : 2 * count + 1]
    weight_in, weight = refs[count], refs[2 * count + 1]
    refs = refs[2 * count + 2 :]
    tables, sends = refs[:count], refs[count : 2 * count]
    send_sem, recv_sem, fs_send, fs_recv, pair_send, pair_recv = refs[2 * count :]
    members = lax.axis_size("fsdp")
    blocks = sends[0].shape[0]
    cap = blocks // members
    member = lax.axis_index("fsdp")
    group = lax.axis_index("dp")
    x, z = group // NZ, lax.rem(group, NZ)
    chips = members // 2
    y, core = member // 2, lax.rem(member, 2)

    def shifted(axis, delta):
        if axis == "x":
            return {"dp": dp_at(lax.rem(x + delta + NX, NX), z)}
        if axis == "z":
            return {"dp": dp_at(x, lax.rem(z + delta + NZ, NZ))}
        return {"fsdp": lax.rem(y + delta + chips, chips) * 2 + core}

    barrier = pltpu.get_barrier_semaphore()
    for axis in ("x", "z"):
        for delta in (1, -1):
            pl.semaphore_signal(
                barrier, inc=1, device_id=shifted(axis, delta),
                device_id_type=pl.DeviceIdType.MESH,
            )
    for off in range(1, members):
        pl.semaphore_signal(
            barrier, inc=1, device_id={"fsdp": lax.rem(member + off, members)},
            device_id_type=pl.DeviceIdType.MESH,
        )
    for c, (_, order) in enumerate(GATHER_CHUNKS):
        minor_n = NZ if order == "zx" else NX
        major, minor = (x, z) if order == "zx" else (z, x)
        tables[c][pl.ds((major * minor_n + minor) * own, own)] = shards[c][...]
    weight[pl.ds(member * 2, 2)] = weight_in[...]
    pl.semaphore_wait(barrier, 4 + members - 1)

    pending = []
    used = [0]

    def mover(table, axis):
        def send(delta, row, size, row_in):
            k = used[0]
            used[0] += 1
            dst = shifted(axis, delta)
            out = pltpu.make_async_remote_copy(
                src_ref=table.at[pl.ds(row, size)], dst_ref=table.at[pl.ds(row, size)],
                send_sem=send_sem.at[k], recv_sem=recv_sem.at[k],
                device_id=dst, device_id_type=pl.DeviceIdType.MESH,
            )
            out.start()
            pending.append(out)
            landed = pltpu.make_async_remote_copy(
                src_ref=table.at[pl.ds(row_in, size)], dst_ref=table.at[pl.ds(row_in, size)],
                send_sem=send_sem.at[k], recv_sem=recv_sem.at[k],
                device_id=dst, device_id_type=pl.DeviceIdType.MESH,
            )
            return landed.wait_recv

        return send

    def chunk_flow(c, order):
        table = tables[c]
        first, second = order
        n1, n2 = (NZ, NX) if order == "zx" else (NX, NZ)
        minor, major = (z, x) if order == "zx" else (x, z)
        yield from ring(
            mover(table, first), n1, minor, own, lambda i: (major * n1 + i) * own
        )
        yield from ring(mover(table, second), n2, major, n1 * own, lambda i: i * n1 * own)

        def pick(b, carry):
            sends[c][pl.ds(b, 1)] = table[pl.ds(slot_ref[c * blocks + b], 1)]
            return carry

        lax.fori_loop(0, blocks, pick, 0)
        outs[c][pl.ds(member * cap, cap)] = sends[c][pl.ds(member * cap, cap)]
        for off in range(1, members):
            peer = lax.rem(member + off, members)
            k = c * members + off
            out = pltpu.make_async_remote_copy(
                src_ref=sends[c].at[pl.ds(peer * cap, cap)],
                dst_ref=outs[c].at[pl.ds(member * cap, cap)],
                send_sem=fs_send.at[k], recv_sem=fs_recv.at[k],
                device_id={"fsdp": peer}, device_id_type=pl.DeviceIdType.MESH,
            )
            out.start()
            pending.append(out)

    pair_waits = []

    def to_other_core(i, lo, hi):
        k = len(pair_waits)
        peer = {"fsdp": y * 2 + 1 - core}
        rows = lambda which: weight.at[pl.ds((i * 2 + which) * 2 + lo, hi - lo)]
        copies = [
            pltpu.make_async_remote_copy(
                src_ref=rows(which), dst_ref=rows(which),
                send_sem=pair_send.at[k], recv_sem=pair_recv.at[k],
                device_id=peer, device_id_type=pl.DeviceIdType.MESH,
            )
            for which in (core, 1 - core)
        ]
        copies[0].start()
        pending.append(copies[0])
        pair_waits.append(copies[1].wait_recv)

    def weight_flow():
        to_other_core(y, 0, 2)
        yield from ring(
            mover(weight, "y"), chips, y, 2, lambda i: (i * 2 + core) * 2, to_other_core
        )

    flows = [chunk_flow(c, order) for c, (_, order) in enumerate(GATHER_CHUNKS)]
    flows.append(weight_flow())
    for flow in flows:
        next(flow)
    for turn in FLOW_ORDER:
        next(flows[turn], None)
    for flow in flows:
        assert next(flow, None) is None
    for wait in pair_waits:
        wait()
    for c in range(count):
        for off in range(1, members):
            source = lax.rem(member - off + members, members)
            k = c * members + off
            pltpu.make_async_remote_copy(
                src_ref=sends[c].at[pl.ds(source * cap, cap)],
                dst_ref=outs[c].at[pl.ds(source * cap, cap)],
                send_sem=fs_send.at[k], recv_sem=fs_recv.at[k],
                device_id={"fsdp": source}, device_id_type=pl.DeviceIdType.MESH,
            ).wait_recv()
    for copy in pending:
        copy.wait_send()


def gather_adapters(packed, base_weight, slot_tab, members, cap):
    own = packed.shape[0]
    tenants = own * NX * NZ
    count = len(GATHER_CHUNKS)
    blocks = members * cap
    shards, start = [], 0
    for rows, _ in GATHER_CHUNKS:
        shards.append(packed[:, start : start + rows])
        start += rows
    vmem = pl.BlockSpec(memory_space=pltpu.VMEM)
    moves = count * 2 * (NX // 2 + NZ // 2) + members // 2
    depth, width = base_weight.shape
    halves = base_weight.reshape(2, depth // 2, width)
    outs = pl.pallas_call(
        functools.partial(gather_kernel, own),
        out_shape=[
            jax.ShapeDtypeStruct((blocks, rows, LANES), jnp.bfloat16) for rows, _ in GATHER_CHUNKS
        ]
        + [jax.ShapeDtypeStruct((members * 2, depth // 2, width), jnp.bfloat16)],
        in_specs=[pl.BlockSpec(memory_space=pltpu.SMEM)] + [vmem] * (count + 1),
        out_specs=[vmem] * (count + 1),
        scratch_shapes=[pltpu.VMEM((tenants, rows, LANES), jnp.bfloat16) for rows, _ in GATHER_CHUNKS]
        + [pltpu.VMEM((blocks, rows, LANES), jnp.bfloat16) for rows, _ in GATHER_CHUNKS]
        + [
            pltpu.SemaphoreType.DMA((moves,)),
            pltpu.SemaphoreType.DMA((moves,)),
            pltpu.SemaphoreType.DMA((count * members,)),
            pltpu.SemaphoreType.DMA((count * members,)),
            pltpu.SemaphoreType.DMA((members + 1,)),
            pltpu.SemaphoreType.DMA((members + 1,)),
        ],
        compiler_params=pltpu.CompilerParams(
            collective_id=0, has_side_effects=True, vmem_limit_bytes=VMEM_LIMIT
        ),
        name="gather_adapters",
    )(slot_tab, *shards, halves)
    return outs[:count], outs[count].reshape(members * depth, width)


def scatter_kernel(own, tab, *refs):
    count = len(SCATTER_CHUNKS)
    take = lambda i: refs[i * count : (i + 1) * count]
    grads, outs, lands, runs, sends1, lands1, sends2, lands2 = (take(i) for i in range(8))
    fs_send, fs_recv, s1_send, s1_recv, s2_send, s2_recv = refs[8 * count :]
    members = lax.axis_size("fsdp")
    blocks = grads[0].shape[0]
    cap = blocks // members
    pairs = NX * NZ * SLOTS
    sums = NX * NZ * own
    member = lax.axis_index("fsdp")
    group = lax.axis_index("dp")
    x, z = group // NZ, lax.rem(group, NZ)
    mesh_ids = pl.DeviceIdType.MESH
    at_x = lambda i: {"dp": dp_at(i, z)}
    at_z = lambda i: {"dp": dp_at(x, i)}

    barrier = pltpu.get_barrier_semaphore()
    for off in range(1, members):
        pl.semaphore_signal(
            barrier, inc=1, device_id={"fsdp": lax.rem(member + off, members)},
            device_id_type=mesh_ids,
        )
    for off in range(1, NX):
        pl.semaphore_signal(
            barrier, inc=1, device_id=at_x(lax.rem(x + off, NX)), device_id_type=mesh_ids
        )
    for off in range(1, NZ):
        pl.semaphore_signal(
            barrier, inc=1, device_id=at_z(lax.rem(z + off, NZ)), device_id_type=mesh_ids
        )
    pl.semaphore_wait(barrier, members - 1 + NX - 1 + NZ - 1)

    pending = []

    def exchange(src, dst, n, me, rows, target, send_sem, recv_sem, base):
        waits = []
        for off in range(1, n):
            peer = lax.rem(me + off, n)
            source = lax.rem(me - off + n, n)
            copy = pltpu.make_async_remote_copy(
                src_ref=src.at[pl.ds(peer * rows, rows)], dst_ref=dst.at[pl.ds(me * rows, rows)],
                send_sem=send_sem.at[base + off], recv_sem=recv_sem.at[base + off],
                device_id=target(peer), device_id_type=mesh_ids,
            )
            copy.start()
            pending.append(copy)
            waits.append(
                pltpu.make_async_remote_copy(
                    src_ref=src.at[pl.ds(source * rows, rows)],
                    dst_ref=dst.at[pl.ds(source * rows, rows)],
                    send_sem=send_sem.at[base + off], recv_sem=recv_sem.at[base + off],
                    device_id=target(source), device_id_type=mesh_ids,
                ).wait_recv
            )
        dst[pl.ds(me * rows, rows)] = src[pl.ds(me * rows, rows)]
        return waits

    fs_waits = [
        exchange(
            grads[c], lands[c], members, member, cap, lambda i: {"fsdp": i}, fs_send, fs_recv,
            c * members,
        )
        for c in range(count)
    ]
    waits1, waits2 = [], []

    def first_stage(c, order):
        n1, first = (NX, x) if order[0] == "x" else (NZ, z)
        target = at_x if order[0] == "x" else at_z
        kind = blocks + (0 if order[0] == "x" else pairs)
        run, send, land1 = runs[c], sends1[c], lands1[c]
        run[pl.ds(blocks, 1)] = jnp.zeros((1,) + run.shape[1:], run.dtype)
        land1[pl.ds(pairs, 1)] = jnp.zeros((1,) + land1.shape[1:], land1.dtype)
        for wait in fs_waits[c]:
            wait()

        def add(b, carry, run=run, land=lands[c]):
            run[pl.ds(b, 1)] = land[pl.ds(b, 1)].astype(jnp.float32) + run[pl.ds(tab[b], 1)]
            return carry

        lax.fori_loop(0, blocks, add, 0)

        def pick(p, carry, run=run, send=send, kind=kind):
            send[pl.ds(p, 1)] = run[pl.ds(tab[kind + p], 1)].astype(jnp.bfloat16)
            return carry

        lax.fori_loop(0, pairs, pick, 0)
        waits1.append(
            exchange(send, land1, n1, first, pairs // n1, target, s1_send, s1_recv, c * NZ)
        )

    def second_stage(c, order):
        n1, n2, second = (NX, NZ, z) if order[0] == "x" else (NZ, NX, x)
        target = at_z if order[0] == "x" else at_x
        kind = blocks + 2 * pairs + (0 if order[0] == "x" else sums)
        for wait in waits1[c]:
            wait()

        def total(q, carry, n1=n1, n2=n2, kind=kind, land1=lands1[c], send2=sends2[c]):
            acc = land1[pl.ds(tab[kind + q], 1)].astype(jnp.float32)
            for f in range(1, n1):
                acc = acc + land1[pl.ds(tab[kind + f * (n2 * own) + q], 1)].astype(jnp.float32)
            send2[pl.ds(q, 1)] = acc.astype(jnp.bfloat16)
            return carry

        lax.fori_loop(0, n2 * own, total, 0)
        waits2.append(
            exchange(sends2[c], lands2[c], n2, second, own, target, s2_send, s2_recv, c * NZ)
        )

    for c, (_, order) in enumerate(SCATTER_CHUNKS):
        first_stage(c, order)
        if c > 0:
            second_stage(c - 1, SCATTER_CHUNKS[c - 1][1])
    second_stage(count - 1, SCATTER_CHUNKS[-1][1])
    for c, (_, order) in enumerate(SCATTER_CHUNKS):
        n2 = NZ if order[0] == "x" else NX
        for wait in waits2[c]:
            wait()
        for j in range(own):
            acc = lands2[c][j].astype(jnp.float32)
            for s in range(1, n2):
                acc = acc + lands2[c][s * own + j].astype(jnp.float32)
            outs[c][j] = acc
    for copy in pending:
        copy.wait_send()


def scatter_gradients(packed, tab, own, members):
    count = len(SCATTER_CHUNKS)
    blocks = packed.shape[0]
    pairs = NX * NZ * SLOTS
    grads, start = [], 0
    for rows, _ in SCATTER_CHUNKS:
        grads.append(packed[:, start : start + rows])
        start += rows
    vmem = pl.BlockSpec(memory_space=pltpu.VMEM)
    bf, f32 = jnp.bfloat16, jnp.float32
    second = [(NZ if order[0] == "x" else NX) * own for _, order in SCATTER_CHUNKS]
    buffers = lambda sizes, kind: [
        pltpu.VMEM((size, rows, LANES), kind) for size, (rows, _) in zip(sizes, SCATTER_CHUNKS)
    ]
    outs = pl.pallas_call(
        functools.partial(scatter_kernel, own),
        out_shape=[jax.ShapeDtypeStruct((own, rows, LANES), f32) for rows, _ in SCATTER_CHUNKS],
        in_specs=[pl.BlockSpec(memory_space=pltpu.SMEM)] + [vmem] * count,
        out_specs=[vmem] * count,
        scratch_shapes=buffers([blocks] * count, bf)
        + buffers([blocks + 1] * count, f32)
        + buffers([pairs] * count, bf)
        + buffers([pairs + 1] * count, bf)
        + buffers(second, bf)
        + buffers(second, bf)
        + [pltpu.SemaphoreType.DMA((count * members,))] * 2
        + [pltpu.SemaphoreType.DMA((count * NZ,))] * 4,
        compiler_params=pltpu.CompilerParams(
            collective_id=1, has_side_effects=True, vmem_limit_bytes=VMEM_LIMIT
        ),
        name="scatter_gradients",
    )(tab, *grads)
    return jnp.concatenate(outs, axis=1)


def lane_rows(array):
    lead, (rows, width) = array.shape[:-2], array.shape[-2:]
    parts = array.reshape(lead + (rows, width // LANES, LANES))
    return jnp.swapaxes(parts, -3, -2).reshape(lead + (rows * width // LANES, LANES))


def from_lane_rows(array, rows):
    lead, count = array.shape[:-2], array.shape[-2] // rows
    parts = array.reshape(lead + (count, rows, LANES))
    return jnp.swapaxes(parts, -3, -2).reshape(lead + (rows, count * LANES))


def pack(down, up):
    parts = jnp.concatenate([lane_rows(down), lane_rows(up)], axis=-2)
    room = PIECE - parts.shape[-2]
    return jnp.pad(parts, [(0, 0)] * (parts.ndim - 2) + [(0, room), (0, 0)])


def local(
    tokens,
    base_weight,
    cotangent,
    tenant_of_block,
    slot_of_tenant,
    live_blocks,
    down_param,
    down_mom,
    down_var,
    up_param,
    up_mom,
    up_var,
):
    groups = lax.axis_size("dp")
    members = lax.axis_size("fsdp")
    own_count = down_param.shape[0]
    tenants = own_count * groups
    seg_total = tenant_of_block.shape[0]
    segment_capacity = seg_total // (groups * members)
    block_row_count = tokens.shape[0] // segment_capacity
    feat_width = tokens.shape[1]
    heads_weight = base_weight.shape[1]
    rank_sh = down_param.shape[1]
    me_group = lax.axis_index("dp")
    me_member = lax.axis_index("fsdp")
    highest = lax.Precision.HIGHEST
    tenant_range = jnp.arange(tenants, dtype=jnp.int32)
    block_slot = jnp.sum(
        jnp.where(tenant_of_block[:, None] == tenant_range[None, :], slot_of_tenant[None, :], 0),
        axis=1,
    )
    block_group = jnp.arange(seg_total, dtype=jnp.int32) // segment_capacity % groups
    slot_onehot = (block_slot[:, None] == tenant_range[None, :]).astype(jnp.float32)
    group_onehot = (block_group[:, None] == jnp.arange(groups, dtype=jnp.int32)[None, :]).astype(
        jnp.float32
    )
    need_count = jnp.dot(group_onehot.T, slot_onehot, precision=highest)
    need_int = (need_count > 0.5).astype(jnp.int32).reshape(groups, groups, own_count)
    rank_tab = jnp.cumsum(need_int, axis=2) - need_int
    rank_rows = jnp.dot(
        group_onehot, rank_tab.reshape(groups, tenants).astype(jnp.float32), precision=highest
    )
    block_rank = jnp.sum(rank_rows * slot_onehot, axis=1).astype(jnp.int32)
    block_pos = block_slot // own_count * SLOTS + block_rank
    group_blocks = (
        jnp.arange(members, dtype=jnp.int32)[:, None] * groups + me_group
    ) * segment_capacity + jnp.arange(segment_capacity, dtype=jnp.int32)[None, :]
    pick_pos = jnp.take(block_pos, group_blocks, axis=0).reshape(-1)
    table_pick = jnp.take(block_slot, group_blocks, axis=0).reshape(-1)
    pick_xz = table_pick
    owner = table_pick // own_count
    pick_zx = (owner % NZ * NX + owner // NZ) * own_count + table_pick % own_count
    slot_tab = jnp.concatenate(
        [pick_xz if order == "zx" else pick_zx for _, order in GATHER_CHUNKS]
    )
    down_used = down_param.astype(jnp.bfloat16)
    up_used = up_param.astype(jnp.bfloat16)
    pieces, full_weight = gather_adapters(
        pack(down_used, up_used), base_weight, slot_tab, members, segment_capacity
    )
    pieces = jnp.concatenate(pieces, axis=1)
    down_rows = rank_sh * feat_width // LANES
    up_rows = rank_sh * heads_weight // LANES
    by_rank = lambda rows: jnp.swapaxes(
        from_lane_rows(rows, rank_sh).reshape(members, segment_capacity, rank_sh, -1), 0, 1
    ).reshape(segment_capacity, members * rank_sh, -1)
    block_down = by_rank(pieces[:, :down_rows])
    block_up = by_rank(pieces[:, down_rows : down_rows + up_rows])
    own_blocks = members * segment_capacity
    place = jnp.arange(own_blocks, dtype=jnp.int32)
    same = (pick_pos[:, None] == pick_pos[None, :]) & (place[None, :] < place[:, None])
    earlier = jnp.max(jnp.where(same, place[None, :], -1), axis=1)
    earlier = jnp.where(earlier < 0, own_blocks, earlier)
    pair_range = jnp.arange(groups * SLOTS, dtype=jnp.int32)
    final = jnp.max(jnp.where(pick_pos[None, :] == pair_range[:, None], place[None, :], -1), axis=1)
    final = jnp.where(final < 0, own_blocks, final)
    final_zx = jnp.swapaxes(final.reshape(NX, NZ, SLOTS), 0, 1).reshape(-1)
    rank_or = jnp.where(need_int == 1, rank_tab, -1).reshape(NX, NZ, NX, NZ, own_count)
    me_x, me_z = me_group // NZ, me_group % NZ
    to_x = jnp.take(jnp.take(rank_or, me_z, axis=1), me_x, axis=1)
    to_z = jnp.take(jnp.take(rank_or, me_x, axis=0), me_z, axis=2)

    def landed(ranks):
        first, second, _ = ranks.shape
        base = jnp.arange(first * second, dtype=jnp.int32).reshape(first, second, 1) * SLOTS
        return jnp.where(ranks >= 0, base + ranks, groups * SLOTS).reshape(-1)

    sum_tab = jnp.concatenate([earlier, final, final_zx, landed(to_x), landed(to_z)])
    frozen_output = jnp.dot(
        tokens,
        full_weight,
        preferred_element_type=jnp.float32,
    )
    my_device = me_member * groups + me_group
    live_count = live_blocks[my_device]
    live_mask = (jnp.arange(segment_capacity, dtype=jnp.int32) < live_count)[:, None, None]
    blocks = tokens.reshape(segment_capacity, block_row_count, feat_width)
    hidden_state = jnp.einsum(
        "cbx,crx->cbr", blocks, block_down, preferred_element_type=jnp.float32
    ).astype(jnp.bfloat16)
    adapter_output = jnp.einsum(
        "cbr,crk->cbk", hidden_state, block_up, preferred_element_type=jnp.float32
    )
    key_blocks = jnp.where(
        live_mask,
        frozen_output.reshape(segment_capacity, block_row_count, heads_weight)
        + adapter_scale * adapter_output,
        jnp.float32(0.0),
    )
    key_proj = key_blocks.astype(jnp.bfloat16).reshape(tokens.shape[0], heads_weight)
    cot_blocks = cotangent.reshape(segment_capacity, block_row_count, heads_weight)
    cotangent_active = jnp.where(live_mask, cot_blocks, jnp.zeros_like(cot_blocks))
    up_gradient = (
        adapter_scale
        * jnp.einsum(
            "cbr,cbk->crk", hidden_state, cotangent_active, preferred_element_type=jnp.float32
        )
    ).astype(jnp.bfloat16)
    hidden_gradient = (
        adapter_scale
        * jnp.einsum("cbk,crk->cbr", cotangent_active, block_up, preferred_element_type=jnp.float32)
    ).astype(jnp.bfloat16)
    grad_down = jnp.einsum(
        "cbr,cbx->crx", hidden_gradient, blocks, preferred_element_type=jnp.float32
    ).astype(jnp.bfloat16)
    by_member = lambda rows: jnp.swapaxes(
        rows.reshape(segment_capacity, members, rank_sh, -1), 0, 1
    ).reshape(own_blocks, rank_sh, -1)
    grad_rows = pack(by_member(grad_down), by_member(up_gradient))
    sum_rows = scatter_gradients(grad_rows, sum_tab, own_count, members)
    sum_down = from_lane_rows(sum_rows[:, :down_rows], rank_sh)
    sum_up = from_lane_rows(sum_rows[:, down_rows : down_rows + up_rows], rank_sh)
    new_down, new_down_mom, new_down_var = adam_update(down_param, down_mom, down_var, sum_down)
    new_up, new_up_mom, new_up_var = adam_update(up_param, up_mom, up_var, sum_up)
    return (key_proj, new_down, new_down_mom, new_down_var, new_up, new_up_mom, new_up_var)


def solution(mesh):
    return jax.shard_map(
        local,
        mesh=mesh,
        in_specs=(
            P(("fsdp", "dp"), None),
            P("fsdp", None),
            P(("fsdp", "dp"), None),
            P(),
            P(),
            P(),
            P("dp", "fsdp", None),
            P("dp", "fsdp", None),
            P("dp", "fsdp", None),
            P("dp", "fsdp", None),
            P("dp", "fsdp", None),
            P("dp", "fsdp", None),
        ),
        out_specs=(
            P(("fsdp", "dp"), None),
            P("dp", "fsdp", None),
            P("dp", "fsdp", None),
            P("dp", "fsdp", None),
            P("dp", "fsdp", None),
            P("dp", "fsdp", None),
            P("dp", "fsdp", None),
        ),
        check_vma=False,
    )
```

```python
import functools

import jax
import jax.numpy as jnp
from jax import lax
from jax.experimental import pallas as pl
from jax.experimental.pallas import tpu as pltpu
from jax.sharding import PartitionSpec as P

SLOTS = 2
LANES = 128
NX, NZ = 4, 8
GATHER_CHUNKS = ((32, "zx"), (32, "xz"), (48, "zx"), (48, "xz"))
SCATTER_CHUNKS = ((32, "zx"), (48, "xz"), (48, "xz"), (32, "xz"))
FLOW_ORDER = (0, 1) * 3 + (2, 3, 0, 1) * 3 + (2, 3) * 3
PIECE = 160
VMEM_LIMIT = 60 * 1024 * 1024


adapter_scale = 2.0
learn_rate = 0.01
beta_one = 0.9
beta_two = 0.99
adam_eps = 1e-08
correct_one = 1.0 - 0.9**8
correct_two = 1.0 - 0.99**8


def adam_update(master, moment, second, gradient):
    moment_new = beta_one * moment + (1.0 - beta_one) * gradient
    second_new = beta_two * second + (1.0 - beta_two) * gradient * gradient
    master_new = master - learn_rate * (moment_new / correct_one) / (
        jnp.sqrt(second_new / correct_two) + adam_eps
    )
    return (master_new, moment_new, second_new)


def dp_at(x, z):
    return x * NZ + z


def ring(send, n, me, unit, row_of, arrived=None):
    half = (unit + 1) // 2
    for step in range(1, n // 2 + 1):
        last = step == n // 2
        lo = (0, half if last else unit)
        hi = (half if last else 0, unit)
        out_r = row_of(lax.rem(me - (step - 1) + n, n))
        out_l = row_of(lax.rem(me + (step - 1), n))
        in_r = row_of(lax.rem(me - step + n, n))
        in_l = row_of(lax.rem(me + step, n))
        wait_r = send(+1, out_r + lo[0], lo[1] - lo[0], in_r + lo[0])
        wait_l = send(-1, out_l + hi[0], hi[1] - hi[0], in_l + hi[0])
        yield
        wait_r()
        wait_l()
        if arrived is not None:
            arrived(lax.rem(me - step + n, n), *lo)
            arrived(lax.rem(me + step, n), *hi)


def gather_kernel(own, slot_ref, *refs):
    count = len(GATHER_CHUNKS)
    shards, outs = refs[:count], refs[count : 2 * count]
    tables, sends = refs[2 * count : 3 * count], refs[3 * count : 4 * count]
    send_sem, recv_sem, fs_send, fs_recv = refs[4 * count :]
    members = lax.axis_size("fsdp")
    blocks = sends[0].shape[0]
    cap = blocks // members
    member = lax.axis_index("fsdp")
    group = lax.axis_index("dp")
    x, z = group // NZ, lax.rem(group, NZ)

    def shifted(axis, delta):
        if axis == "x":
            return {"dp": dp_at(lax.rem(x + delta + NX, NX), z)}
        return {"dp": dp_at(x, lax.rem(z + delta + NZ, NZ))}

    barrier = pltpu.get_barrier_semaphore()
    for axis in ("x", "z"):
        for delta in (1, -1):
            pl.semaphore_signal(
                barrier, inc=1, device_id=shifted(axis, delta),
                device_id_type=pl.DeviceIdType.MESH,
            )
    for off in range(1, members):
        pl.semaphore_signal(
            barrier, inc=1, device_id={"fsdp": lax.rem(member + off, members)},
            device_id_type=pl.DeviceIdType.MESH,
        )
    for c, (_, order) in enumerate(GATHER_CHUNKS):
        minor_n = NZ if order == "zx" else NX
        major, minor = (x, z) if order == "zx" else (z, x)
        tables[c][pl.ds((major * minor_n + minor) * own, own)] = shards[c][...]
    pl.semaphore_wait(barrier, 4 + members - 1)

    pending = []
    used = [0]

    def mover(table, axis):
        def send(delta, row, size, row_in):
            k = used[0]
            used[0] += 1
            dst = shifted(axis, delta)
            out = pltpu.make_async_remote_copy(
                src_ref=table.at[pl.ds(row, size)], dst_ref=table.at[pl.ds(row, size)],
                send_sem=send_sem.at[k], recv_sem=recv_sem.at[k],
                device_id=dst, device_id_type=pl.DeviceIdType.MESH,
            )
            out.start()
            pending.append(out)
            landed = pltpu.make_async_remote_copy(
                src_ref=table.at[pl.ds(row_in, size)], dst_ref=table.at[pl.ds(row_in, size)],
                send_sem=send_sem.at[k], recv_sem=recv_sem.at[k],
                device_id=dst, device_id_type=pl.DeviceIdType.MESH,
            )
            return landed.wait_recv

        return send

    def chunk_flow(c, order):
        table = tables[c]
        first, second = order
        n1, n2 = (NZ, NX) if order == "zx" else (NX, NZ)
        minor, major = (z, x) if order == "zx" else (x, z)
        yield from ring(
            mover(table, first), n1, minor, own, lambda i: (major * n1 + i) * own
        )
        yield from ring(mover(table, second), n2, major, n1 * own, lambda i: i * n1 * own)

        def pick(b, carry):
            sends[c][pl.ds(b, 1)] = table[pl.ds(slot_ref[c * blocks + b], 1)]
            return carry

        lax.fori_loop(0, blocks, pick, 0)
        outs[c][pl.ds(member * cap, cap)] = sends[c][pl.ds(member * cap, cap)]
        for off in range(1, members):
            peer = lax.rem(member + off, members)
            k = c * members + off
            out = pltpu.make_async_remote_copy(
                src_ref=sends[c].at[pl.ds(peer * cap, cap)],
                dst_ref=outs[c].at[pl.ds(member * cap, cap)],
                send_sem=fs_send.at[k], recv_sem=fs_recv.at[k],
                device_id={"fsdp": peer}, device_id_type=pl.DeviceIdType.MESH,
            )
            out.start()
            pending.append(out)

    flows = [chunk_flow(c, order) for c, (_, order) in enumerate(GATHER_CHUNKS)]
    for flow in flows:
        next(flow)
    for turn in FLOW_ORDER:
        next(flows[turn], None)
    for c in range(count):
        for off in range(1, members):
            source = lax.rem(member - off + members, members)
            k = c * members + off
            pltpu.make_async_remote_copy(
                src_ref=sends[c].at[pl.ds(source * cap, cap)],
                dst_ref=outs[c].at[pl.ds(source * cap, cap)],
                send_sem=fs_send.at[k], recv_sem=fs_recv.at[k],
                device_id={"fsdp": source}, device_id_type=pl.DeviceIdType.MESH,
            ).wait_recv()
    for copy in pending:
        copy.wait_send()


def gather_adapters(packed, slot_tab, members, cap):
    own = packed.shape[0]
    tenants = own * NX * NZ
    count = len(GATHER_CHUNKS)
    blocks = members * cap
    shards, start = [], 0
    for rows, _ in GATHER_CHUNKS:
        shards.append(packed[:, start : start + rows])
        start += rows
    vmem = pl.BlockSpec(memory_space=pltpu.VMEM)
    moves = count * 2 * (NX // 2 + NZ // 2)
    return pl.pallas_call(
        functools.partial(gather_kernel, own),
        out_shape=[
            jax.ShapeDtypeStruct((blocks, rows, LANES), jnp.bfloat16) for rows, _ in GATHER_CHUNKS
        ],
        in_specs=[pl.BlockSpec(memory_space=pltpu.SMEM)] + [vmem] * count,
        out_specs=[vmem] * count,
        scratch_shapes=[pltpu.VMEM((tenants, rows, LANES), jnp.bfloat16) for rows, _ in GATHER_CHUNKS]
        + [pltpu.VMEM((blocks, rows, LANES), jnp.bfloat16) for rows, _ in GATHER_CHUNKS]
        + [
            pltpu.SemaphoreType.DMA((moves,)),
            pltpu.SemaphoreType.DMA((moves,)),
            pltpu.SemaphoreType.DMA((count * members,)),
            pltpu.SemaphoreType.DMA((count * members,)),
        ],
        compiler_params=pltpu.CompilerParams(
            collective_id=0, has_side_effects=True, vmem_limit_bytes=VMEM_LIMIT
        ),
        name="gather_adapters",
    )(slot_tab, *shards)


def scatter_kernel(own, tab, tokens, weight_in, adapter, *refs):
    count = len(SCATTER_CHUNKS)
    key = refs[2 * count]
    refs = refs[: 2 * count] + refs[2 * count + 1 :]
    take = lambda i: refs[i * count : (i + 1) * count]
    grads, outs, lands, runs, sends1, lands1, sends2, lands2 = (take(i) for i in range(8))
    weight, frozen, fs_send, fs_recv, s1_send, s1_recv, s2_send, s2_recv = refs[
        8 * count : 8 * count + 8
    ]
    ring_send, ring_recv, pair_send, pair_recv = refs[8 * count + 8 :]
    members = lax.axis_size("fsdp")
    blocks = grads[0].shape[0]
    cap = blocks // members
    pairs = NX * NZ * SLOTS
    sums = NX * NZ * own
    member = lax.axis_index("fsdp")
    group = lax.axis_index("dp")
    x, z = group // NZ, lax.rem(group, NZ)
    mesh_ids = pl.DeviceIdType.MESH
    chips = members // 2
    y, core = member // 2, lax.rem(member, 2)
    at_x = lambda i: {"dp": dp_at(i, z)}
    at_z = lambda i: {"dp": dp_at(x, i)}

    barrier = pltpu.get_barrier_semaphore()
    for off in range(1, members):
        pl.semaphore_signal(
            barrier, inc=1, device_id={"fsdp": lax.rem(member + off, members)},
            device_id_type=mesh_ids,
        )
    for off in range(1, NX):
        pl.semaphore_signal(
            barrier, inc=1, device_id=at_x(lax.rem(x + off, NX)), device_id_type=mesh_ids
        )
    for off in range(1, NZ):
        pl.semaphore_signal(
            barrier, inc=1, device_id=at_z(lax.rem(z + off, NZ)), device_id_type=mesh_ids
        )
    weight[pl.ds(member * 2, 2)] = weight_in[...]
    pl.semaphore_wait(barrier, members - 1 + NX - 1 + NZ - 1)

    pending = []

    def exchange(src, dst, n, me, rows, target, send_sem, recv_sem, base):
        waits = []
        for off in range(1, n):
            peer = lax.rem(me + off, n)
            source = lax.rem(me - off + n, n)
            copy = pltpu.make_async_remote_copy(
                src_ref=src.at[pl.ds(peer * rows, rows)], dst_ref=dst.at[pl.ds(me * rows, rows)],
                send_sem=send_sem.at[base + off], recv_sem=recv_sem.at[base + off],
                device_id=target(peer), device_id_type=mesh_ids,
            )
            copy.start()
            pending.append(copy)
            waits.append(
                pltpu.make_async_remote_copy(
                    src_ref=src.at[pl.ds(source * rows, rows)],
                    dst_ref=dst.at[pl.ds(source * rows, rows)],
                    send_sem=send_sem.at[base + off], recv_sem=recv_sem.at[base + off],
                    device_id=target(source), device_id_type=mesh_ids,
                ).wait_recv
            )
        dst[pl.ds(me * rows, rows)] = src[pl.ds(me * rows, rows)]
        return waits

    fs_waits = [
        exchange(
            grads[c], lands[c], members, member, cap, lambda i: {"fsdp": i}, fs_send, fs_recv,
            c * members,
        )
        for c in range(count)
    ]
    pair_waits = []

    def to_other_core(i, lo, hi):
        k = len(pair_waits)
        peer = {"fsdp": y * 2 + 1 - core}
        rows = lambda which: weight.at[pl.ds((i * 2 + which) * 2 + lo, hi - lo)]
        copies = [
            pltpu.make_async_remote_copy(
                src_ref=rows(which), dst_ref=rows(which),
                send_sem=pair_send.at[k], recv_sem=pair_recv.at[k],
                device_id=peer, device_id_type=pl.DeviceIdType.MESH,
            )
            for which in (core, 1 - core)
        ]
        copies[0].start()
        pending.append(copies[0])
        pair_waits.append(copies[1].wait_recv)

    used = [0]

    def along_y(delta, row, size, row_in):
        k = used[0]
        used[0] += 1
        dst = {"fsdp": lax.rem(y + delta + chips, chips) * 2 + core}
        copies = [
            pltpu.make_async_remote_copy(
                src_ref=weight.at[pl.ds(at, size)], dst_ref=weight.at[pl.ds(at, size)],
                send_sem=ring_send.at[k], recv_sem=ring_recv.at[k],
                device_id=dst, device_id_type=mesh_ids,
            )
            for at in (row, row_in)
        ]
        copies[0].start()
        pending.append(copies[0])
        return copies[1].wait_recv

    weight_flow = ring(along_y, chips, y, 2, lambda i: (i * 2 + core) * 2, to_other_core)

    to_other_core(y, 0, 2)
    next(weight_flow)
    waits1, waits2 = [], []

    def first_stage(c, order):
        n1, first = (NX, x) if order[0] == "x" else (NZ, z)
        target = at_x if order[0] == "x" else at_z
        kind = blocks + (0 if order[0] == "x" else pairs)
        run, send, land1 = runs[c], sends1[c], lands1[c]
        run[pl.ds(blocks, 1)] = jnp.zeros((1,) + run.shape[1:], run.dtype)
        land1[pl.ds(pairs, 1)] = jnp.zeros((1,) + land1.shape[1:], land1.dtype)
        for wait in fs_waits[c]:
            wait()

        def add(b, carry, run=run, land=lands[c]):
            run[pl.ds(b, 1)] = land[pl.ds(b, 1)].astype(jnp.float32) + run[pl.ds(tab[b], 1)]
            return carry

        lax.fori_loop(0, blocks, add, 0)

        def pick(p, carry, run=run, send=send, kind=kind):
            send[pl.ds(p, 1)] = run[pl.ds(tab[kind + p], 1)].astype(jnp.bfloat16)
            return carry

        lax.fori_loop(0, pairs, pick, 0)
        waits1.append(
            exchange(send, land1, n1, first, pairs // n1, target, s1_send, s1_recv, c * NZ)
        )

    def second_stage(c, order):
        n1, n2, second = (NX, NZ, z) if order[0] == "x" else (NZ, NX, x)
        target = at_z if order[0] == "x" else at_x
        kind = blocks + 2 * pairs + (0 if order[0] == "x" else sums)
        for wait in waits1[c]:
            wait()

        def total(q, carry, n1=n1, n2=n2, kind=kind, land1=lands1[c], send2=sends2[c]):
            acc = land1[pl.ds(tab[kind + q], 1)].astype(jnp.float32)
            for f in range(1, n1):
                acc = acc + land1[pl.ds(tab[kind + f * (n2 * own) + q], 1)].astype(jnp.float32)
            send2[pl.ds(q, 1)] = acc.astype(jnp.bfloat16)
            return carry

        lax.fori_loop(0, n2 * own, total, 0)
        waits2.append(
            exchange(sends2[c], lands2[c], n2, second, own, target, s2_send, s2_recv, c * NZ)
        )

    for c, (_, order) in enumerate(SCATTER_CHUNKS):
        first_stage(c, order)
        if c > 0:
            second_stage(c - 1, SCATTER_CHUNKS[c - 1][1])
    next(weight_flow, None)
    second_stage(count - 1, SCATTER_CHUNKS[-1][1])
    for _ in range(chips // 2 - 1):
        next(weight_flow, None)
    for wait in pair_waits:
        wait()
    depth = weight.shape[1]
    frozen[...] = adapter[...]

    def multiply(k, carry):
        columns = pl.ds(pl.multiple_of(k * depth, depth), depth)
        frozen[...] += jnp.dot(tokens[:, columns], weight[k], preferred_element_type=jnp.float32)
        return carry

    lax.fori_loop(0, weight.shape[0], multiply, 0)
    place = lax.broadcasted_iota(jnp.int32, frozen.shape, 0) // (frozen.shape[0] // cap)
    live = tab[blocks + 2 * pairs + 2 * sums]
    key[...] = jnp.where(place < live, frozen[...], 0.0).astype(key.dtype)
    for c, (_, order) in enumerate(SCATTER_CHUNKS):
        n2 = NZ if order[0] == "x" else NX
        for wait in waits2[c]:
            wait()
        for j in range(own):
            acc = lands2[c][j].astype(jnp.float32)
            for s in range(1, n2):
                acc = acc + lands2[c][s * own + j].astype(jnp.float32)
            outs[c][j] = acc
    for copy in pending:
        copy.wait_send()


def scatter_gradients(packed, tab, tokens, base_weight, adapter, own, members):
    count = len(SCATTER_CHUNKS)
    blocks = packed.shape[0]
    pairs = NX * NZ * SLOTS
    grads, start = [], 0
    for rows, _ in SCATTER_CHUNKS:
        grads.append(packed[:, start : start + rows])
        start += rows
    vmem = pl.BlockSpec(memory_space=pltpu.VMEM)
    bf, f32 = jnp.bfloat16, jnp.float32
    second = [(NZ if order[0] == "x" else NX) * own for _, order in SCATTER_CHUNKS]
    buffers = lambda sizes, kind: [
        pltpu.VMEM((size, rows, LANES), kind) for size, (rows, _) in zip(sizes, SCATTER_CHUNKS)
    ]
    depth, width = base_weight.shape
    halves = base_weight.reshape(2, depth // 2, width)
    outs = pl.pallas_call(
        functools.partial(scatter_kernel, own),
        out_shape=[jax.ShapeDtypeStruct((own, rows, LANES), f32) for rows, _ in SCATTER_CHUNKS]
        + [jax.ShapeDtypeStruct(adapter.shape, bf)],
        in_specs=[pl.BlockSpec(memory_space=pltpu.SMEM)] + [vmem] * (count + 3),
        out_specs=[vmem] * (count + 1),
        scratch_shapes=buffers([blocks] * count, bf)
        + buffers([blocks + 1] * count, f32)
        + buffers([pairs] * count, bf)
        + buffers([pairs + 1] * count, bf)
        + buffers(second, bf)
        + buffers(second, bf)
        + [pltpu.VMEM((members * 2, depth // 2, width), bf), pltpu.VMEM(adapter.shape, f32)]
        + [pltpu.SemaphoreType.DMA((count * members,))] * 2
        + [pltpu.SemaphoreType.DMA((count * NZ,))] * 4
        + [pltpu.SemaphoreType.DMA((members // 2,))] * 2
        + [pltpu.SemaphoreType.DMA((members + 1,))] * 2,
        compiler_params=pltpu.CompilerParams(
            collective_id=1, has_side_effects=True, vmem_limit_bytes=VMEM_LIMIT
        ),
        name="scatter_gradients",
    )(tab, tokens, halves, adapter, *grads)
    return jnp.concatenate(outs[:count], axis=1), outs[count]


def lane_rows(array):
    lead, (rows, width) = array.shape[:-2], array.shape[-2:]
    parts = array.reshape(lead + (rows, width // LANES, LANES))
    return jnp.swapaxes(parts, -3, -2).reshape(lead + (rows * width // LANES, LANES))


def from_lane_rows(array, rows):
    lead, count = array.shape[:-2], array.shape[-2] // rows
    parts = array.reshape(lead + (count, rows, LANES))
    return jnp.swapaxes(parts, -3, -2).reshape(lead + (rows, count * LANES))


def pack(down, up):
    parts = jnp.concatenate([lane_rows(down), lane_rows(up)], axis=-2)
    room = PIECE - parts.shape[-2]
    return jnp.pad(parts, [(0, 0)] * (parts.ndim - 2) + [(0, room), (0, 0)])


def local(
    tokens,
    base_weight,
    cotangent,
    tenant_of_block,
    slot_of_tenant,
    live_blocks,
    down_param,
    down_mom,
    down_var,
    up_param,
    up_mom,
    up_var,
):
    groups = lax.axis_size("dp")
    members = lax.axis_size("fsdp")
    own_count = down_param.shape[0]
    tenants = own_count * groups
    seg_total = tenant_of_block.shape[0]
    segment_capacity = seg_total // (groups * members)
    block_row_count = tokens.shape[0] // segment_capacity
    feat_width = tokens.shape[1]
    heads_weight = base_weight.shape[1]
    rank_sh = down_param.shape[1]
    me_group = lax.axis_index("dp")
    me_member = lax.axis_index("fsdp")
    highest = lax.Precision.HIGHEST
    tenant_range = jnp.arange(tenants, dtype=jnp.int32)
    block_slot = jnp.sum(
        jnp.where(tenant_of_block[:, None] == tenant_range[None, :], slot_of_tenant[None, :], 0),
        axis=1,
    )
    block_group = jnp.arange(seg_total, dtype=jnp.int32) // segment_capacity % groups
    slot_onehot = (block_slot[:, None] == tenant_range[None, :]).astype(jnp.float32)
    group_onehot = (block_group[:, None] == jnp.arange(groups, dtype=jnp.int32)[None, :]).astype(
        jnp.float32
    )
    need_count = jnp.dot(group_onehot.T, slot_onehot, precision=highest)
    need_int = (need_count > 0.5).astype(jnp.int32).reshape(groups, groups, own_count)
    rank_tab = jnp.cumsum(need_int, axis=2) - need_int
    rank_rows = jnp.dot(
        group_onehot, rank_tab.reshape(groups, tenants).astype(jnp.float32), precision=highest
    )
    block_rank = jnp.sum(rank_rows * slot_onehot, axis=1).astype(jnp.int32)
    block_pos = block_slot // own_count * SLOTS + block_rank
    group_blocks = (
        jnp.arange(members, dtype=jnp.int32)[:, None] * groups + me_group
    ) * segment_capacity + jnp.arange(segment_capacity, dtype=jnp.int32)[None, :]
    pick_pos = jnp.take(block_pos, group_blocks, axis=0).reshape(-1)
    table_pick = jnp.take(block_slot, group_blocks, axis=0).reshape(-1)
    pick_xz = table_pick
    owner = table_pick // own_count
    pick_zx = (owner % NZ * NX + owner // NZ) * own_count + table_pick % own_count
    slot_tab = jnp.concatenate(
        [pick_xz if order == "zx" else pick_zx for _, order in GATHER_CHUNKS]
    )
    down_used = down_param.astype(jnp.bfloat16)
    up_used = up_param.astype(jnp.bfloat16)
    pieces = gather_adapters(pack(down_used, up_used), slot_tab, members, segment_capacity)
    pieces = jnp.concatenate(pieces, axis=1)
    down_rows = rank_sh * feat_width // LANES
    up_rows = rank_sh * heads_weight // LANES
    by_rank = lambda rows: jnp.swapaxes(
        from_lane_rows(rows, rank_sh).reshape(members, segment_capacity, rank_sh, -1), 0, 1
    ).reshape(segment_capacity, members * rank_sh, -1)
    block_down = by_rank(pieces[:, :down_rows])
    block_up = by_rank(pieces[:, down_rows : down_rows + up_rows])
    own_blocks = members * segment_capacity
    place = jnp.arange(own_blocks, dtype=jnp.int32)
    same = (pick_pos[:, None] == pick_pos[None, :]) & (place[None, :] < place[:, None])
    earlier = jnp.max(jnp.where(same, place[None, :], -1), axis=1)
    earlier = jnp.where(earlier < 0, own_blocks, earlier)
    pair_range = jnp.arange(groups * SLOTS, dtype=jnp.int32)
    final = jnp.max(jnp.where(pick_pos[None, :] == pair_range[:, None], place[None, :], -1), axis=1)
    final = jnp.where(final < 0, own_blocks, final)
    final_zx = jnp.swapaxes(final.reshape(NX, NZ, SLOTS), 0, 1).reshape(-1)
    rank_or = jnp.where(need_int == 1, rank_tab, -1).reshape(NX, NZ, NX, NZ, own_count)
    me_x, me_z = me_group // NZ, me_group % NZ
    to_x = jnp.take(jnp.take(rank_or, me_z, axis=1), me_x, axis=1)
    to_z = jnp.take(jnp.take(rank_or, me_x, axis=0), me_z, axis=2)

    def landed(ranks):
        first, second, _ = ranks.shape
        base = jnp.arange(first * second, dtype=jnp.int32).reshape(first, second, 1) * SLOTS
        return jnp.where(ranks >= 0, base + ranks, groups * SLOTS).reshape(-1)

    live_count = live_blocks[me_member * groups + me_group]
    sum_tab = jnp.concatenate(
        [earlier, final, final_zx, landed(to_x), landed(to_z), live_count[None]]
    )
    live_mask = (jnp.arange(segment_capacity, dtype=jnp.int32) < live_count)[:, None, None]
    blocks = tokens.reshape(segment_capacity, block_row_count, feat_width)
    hidden_state = jnp.einsum(
        "cbx,crx->cbr", blocks, block_down, preferred_element_type=jnp.float32
    ).astype(jnp.bfloat16)
    adapter_output = jnp.einsum(
        "cbr,crk->cbk", hidden_state, block_up, preferred_element_type=jnp.float32
    )
    adapter_rows = (adapter_scale * adapter_output).reshape(tokens.shape[0], heads_weight)
    cot_blocks = cotangent.reshape(segment_capacity, block_row_count, heads_weight)
    cotangent_active = jnp.where(live_mask, cot_blocks, jnp.zeros_like(cot_blocks))
    up_gradient = (
        adapter_scale
        * jnp.einsum(
            "cbr,cbk->crk", hidden_state, cotangent_active, preferred_element_type=jnp.float32
        )
    ).astype(jnp.bfloat16)
    hidden_gradient = (
        adapter_scale
        * jnp.einsum("cbk,crk->cbr", cotangent_active, block_up, preferred_element_type=jnp.float32)
    ).astype(jnp.bfloat16)
    grad_down = jnp.einsum(
        "cbr,cbx->crx", hidden_gradient, blocks, preferred_element_type=jnp.float32
    ).astype(jnp.bfloat16)
    by_member = lambda rows: jnp.swapaxes(
        rows.reshape(segment_capacity, members, rank_sh, -1), 0, 1
    ).reshape(own_blocks, rank_sh, -1)
    grad_rows = pack(by_member(grad_down), by_member(up_gradient))
    sum_rows, key_proj = scatter_gradients(
        grad_rows, sum_tab, tokens, base_weight, adapter_rows, own_count, members
    )
    sum_down = from_lane_rows(sum_rows[:, :down_rows], rank_sh)
    sum_up = from_lane_rows(sum_rows[:, down_rows : down_rows + up_rows], rank_sh)
    new_down, new_down_mom, new_down_var = adam_update(down_param, down_mom, down_var, sum_down)
    new_up, new_up_mom, new_up_var = adam_update(up_param, up_mom, up_var, sum_up)
    return (key_proj, new_down, new_down_mom, new_down_var, new_up, new_up_mom, new_up_var)


def solution(mesh):
    return jax.shard_map(
        local,
        mesh=mesh,
        in_specs=(
            P(("fsdp", "dp"), None),
            P("fsdp", None),
            P(("fsdp", "dp"), None),
            P(),
            P(),
            P(),
            P("dp", "fsdp", None),
            P("dp", "fsdp", None),
            P("dp", "fsdp", None),
            P("dp", "fsdp", None),
            P("dp", "fsdp", None),
            P("dp", "fsdp", None),
        ),
        out_specs=(
            P(("fsdp", "dp"), None),
            P("dp", "fsdp", None),
            P("dp", "fsdp", None),
            P("dp", "fsdp", None),
            P("dp", "fsdp", None),
            P("dp", "fsdp", None),
            P("dp", "fsdp", None),
        ),
        check_vma=False,
    )
```

```python
import functools

import jax
import jax.numpy as jnp
from jax import lax
from jax.experimental import pallas as pl
from jax.experimental.pallas import tpu as pltpu
from jax.sharding import PartitionSpec as P

SLOTS = 2
LANES = 128
NX, NZ = 4, 8
GATHER_CHUNKS = ((32, "zx"), (32, "xz"), (48, "zx"), (48, "xz"))
SCATTER_CHUNKS = ((32, "zx"), (48, "xz"), (48, "xz"), (32, "xz"))
FLOW_ORDER = (0, 1, 4) * 3 + (2, 3, 0, 1) * 3 + (2, 3) * 3 + (4, 4, 4)
PIECE = 160
VMEM_LIMIT = 60 * 1024 * 1024


adapter_scale = 2.0
learn_rate = 0.01
beta_one = 0.9
beta_two = 0.99
adam_eps = 1e-08
correct_one = 1.0 - 0.9**8
correct_two = 1.0 - 0.99**8


def adam_update(master, moment, second, gradient):
    moment_new = beta_one * moment + (1.0 - beta_one) * gradient
    second_new = beta_two * second + (1.0 - beta_two) * gradient * gradient
    master_new = master - learn_rate * (moment_new / correct_one) / (
        jnp.sqrt(second_new / correct_two) + adam_eps
    )
    return (master_new, moment_new, second_new)


def dp_at(x, z):
    return x * NZ + z


def ring(send, n, me, unit, row_of, arrived=None):
    half = (unit + 1) // 2
    for step in range(1, n // 2 + 1):
        last = step == n // 2
        lo = (0, half if last else unit)
        hi = (half if last else 0, unit)
        out_r = row_of(lax.rem(me - (step - 1) + n, n))
        out_l = row_of(lax.rem(me + (step - 1), n))
        in_r = row_of(lax.rem(me - step + n, n))
        in_l = row_of(lax.rem(me + step, n))
        wait_r = send(+1, out_r + lo[0], lo[1] - lo[0], in_r + lo[0])
        wait_l = send(-1, out_l + hi[0], hi[1] - hi[0], in_l + hi[0])
        yield
        wait_r()
        wait_l()
        if arrived is not None:
            arrived(lax.rem(me - step + n, n), *lo)
            arrived(lax.rem(me + step, n), *hi)


def gather_kernel(own, slot_ref, *refs):
    count = len(GATHER_CHUNKS)
    shards, outs = refs[:count], refs[count + 1 : 2 * count + 1]
    weight_in, weight = refs[count], refs[2 * count + 1]
    refs = refs[2 * count + 2 :]
    tables, sends = refs[:count], refs[count : 2 * count]
    (
        send_sem, recv_sem, fs_send, fs_recv, ring_send, ring_recv, pair_send, pair_recv
    ) = refs[2 * count :]
    members = lax.axis_size("fsdp")
    blocks = sends[0].shape[0]
    cap = blocks // members
    member = lax.axis_index("fsdp")
    group = lax.axis_index("dp")
    x, z = group // NZ, lax.rem(group, NZ)
    chips = members // 2
    y, core = member // 2, lax.rem(member, 2)

    def shifted(axis, delta):
        if axis == "y":
            return {"fsdp": lax.rem(y + delta + chips, chips) * 2 + core}
        if axis == "x":
            return {"dp": dp_at(lax.rem(x + delta + NX, NX), z)}
        return {"dp": dp_at(x, lax.rem(z + delta + NZ, NZ))}

    barrier = pltpu.get_barrier_semaphore()
    for axis in ("x", "z"):
        for delta in (1, -1):
            pl.semaphore_signal(
                barrier, inc=1, device_id=shifted(axis, delta),
                device_id_type=pl.DeviceIdType.MESH,
            )
    for off in range(1, members):
        pl.semaphore_signal(
            barrier, inc=1, device_id={"fsdp": lax.rem(member + off, members)},
            device_id_type=pl.DeviceIdType.MESH,
        )
    for c, (_, order) in enumerate(GATHER_CHUNKS):
        minor_n = NZ if order == "zx" else NX
        major, minor = (x, z) if order == "zx" else (z, x)
        tables[c][pl.ds((major * minor_n + minor) * own, own)] = shards[c][...]
    weight[y, core, x] = weight_in[x]
    pl.semaphore_wait(barrier, 4 + members - 1)

    pending = []
    used = [0]

    def mover(table, axis):
        def send(delta, row, size, row_in):
            k = used[0]
            used[0] += 1
            dst = shifted(axis, delta)
            out = pltpu.make_async_remote_copy(
                src_ref=table.at[pl.ds(row, size)], dst_ref=table.at[pl.ds(row, size)],
                send_sem=send_sem.at[k], recv_sem=recv_sem.at[k],
                device_id=dst, device_id_type=pl.DeviceIdType.MESH,
            )
            out.start()
            pending.append(out)
            landed = pltpu.make_async_remote_copy(
                src_ref=table.at[pl.ds(row_in, size)], dst_ref=table.at[pl.ds(row_in, size)],
                send_sem=send_sem.at[k], recv_sem=recv_sem.at[k],
                device_id=dst, device_id_type=pl.DeviceIdType.MESH,
            )
            return landed.wait_recv

        return send

    def chunk_flow(c, order):
        table = tables[c]
        first, second = order
        n1, n2 = (NZ, NX) if order == "zx" else (NX, NZ)
        minor, major = (z, x) if order == "zx" else (x, z)
        yield from ring(
            mover(table, first), n1, minor, own, lambda i: (major * n1 + i) * own
        )
        yield from ring(mover(table, second), n2, major, n1 * own, lambda i: i * n1 * own)

        def pick(b, carry):
            sends[c][pl.ds(b, 1)] = table[pl.ds(slot_ref[c * blocks + b], 1)]
            return carry

        lax.fori_loop(0, blocks, pick, 0)
        outs[c][pl.ds(member * cap, cap)] = sends[c][pl.ds(member * cap, cap)]
        for off in range(1, members):
            peer = lax.rem(member + off, members)
            k = c * members + off
            out = pltpu.make_async_remote_copy(
                src_ref=sends[c].at[pl.ds(peer * cap, cap)],
                dst_ref=outs[c].at[pl.ds(member * cap, cap)],
                send_sem=fs_send.at[k], recv_sem=fs_recv.at[k],
                device_id={"fsdp": peer}, device_id_type=pl.DeviceIdType.MESH,
            )
            out.start()
            pending.append(out)

    ring_used = [0]
    pair_waits = []

    def weight_copy(here, there, dst, sems, k):
        copies = [
            pltpu.make_async_remote_copy(
                src_ref=at, dst_ref=at, send_sem=sems[0].at[k], recv_sem=sems[1].at[k],
                device_id=dst, device_id_type=pl.DeviceIdType.MESH,
            )
            for at in (here, there)
        ]
        copies[0].start()
        pending.append(copies[0])
        return copies[1].wait_recv

    def weight_mover(axis, part):
        def send(delta, row, size, row_in):
            k = ring_used[0]
            ring_used[0] += 1
            return weight_copy(
                part(row, size), part(row_in, size), shifted(axis, delta), (ring_send, ring_recv), k
            )

        return send

    def to_other_core(i, lo, hi):
        at = lambda which: weight.at[pl.ds(lo, hi - lo), which, i]
        pair_waits.append(
            weight_copy(
                at(core), at(1 - core), {"fsdp": y * 2 + 1 - core}, (pair_send, pair_recv),
                len(pair_waits),
            )
        )

    def weight_flow():
        along_y = lambda row, size: weight.at[row // 2, core, x, pl.ds(lax.rem(row, 2), size)]
        yield from ring(weight_mover("y", along_y), chips, y, 2, lambda i: i * 2)
        to_other_core(x, 0, chips)
        along_x = lambda row, size: weight.at[pl.ds(lax.rem(row, chips), size), core, row // chips]
        yield from ring(
            weight_mover("x", along_x), NX, x, chips, lambda i: i * chips, to_other_core
        )

    flows = [chunk_flow(c, order) for c, (_, order) in enumerate(GATHER_CHUNKS)]
    flows.append(weight_flow())
    for flow in flows:
        next(flow)
    for turn in FLOW_ORDER:
        next(flows[turn], None)
    for wait in pair_waits:
        wait()
    for c in range(count):
        for off in range(1, members):
            source = lax.rem(member - off + members, members)
            k = c * members + off
            pltpu.make_async_remote_copy(
                src_ref=sends[c].at[pl.ds(source * cap, cap)],
                dst_ref=outs[c].at[pl.ds(source * cap, cap)],
                send_sem=fs_send.at[k], recv_sem=fs_recv.at[k],
                device_id={"fsdp": source}, device_id_type=pl.DeviceIdType.MESH,
            ).wait_recv()
    for copy in pending:
        copy.wait_send()


def gather_adapters(packed, base_weight, slot_tab, members, cap):
    own = packed.shape[0]
    tenants = own * NX * NZ
    count = len(GATHER_CHUNKS)
    blocks = members * cap
    shards, start = [], 0
    for rows, _ in GATHER_CHUNKS:
        shards.append(packed[:, start : start + rows])
        start += rows
    vmem = pl.BlockSpec(memory_space=pltpu.VMEM)
    moves = count * 2 * (NX // 2 + NZ // 2)
    depth, width = base_weight.shape
    cut = (NX, 2, depth // NX // 2, width)
    outs = pl.pallas_call(
        functools.partial(gather_kernel, own),
        out_shape=[
            jax.ShapeDtypeStruct((blocks, rows, LANES), jnp.bfloat16) for rows, _ in GATHER_CHUNKS
        ]
        + [jax.ShapeDtypeStruct((members // 2, 2) + cut, jnp.bfloat16)],
        in_specs=[pl.BlockSpec(memory_space=pltpu.SMEM)] + [vmem] * (count + 1),
        out_specs=[vmem] * (count + 1),
        scratch_shapes=[pltpu.VMEM((tenants, rows, LANES), jnp.bfloat16) for rows, _ in GATHER_CHUNKS]
        + [pltpu.VMEM((blocks, rows, LANES), jnp.bfloat16) for rows, _ in GATHER_CHUNKS]
        + [
            pltpu.SemaphoreType.DMA((moves,)),
            pltpu.SemaphoreType.DMA((moves,)),
            pltpu.SemaphoreType.DMA((count * members,)),
            pltpu.SemaphoreType.DMA((count * members,)),
            pltpu.SemaphoreType.DMA((members // 2 + NX,)),
            pltpu.SemaphoreType.DMA((members // 2 + NX,)),
            pltpu.SemaphoreType.DMA((1 + NX,)),
            pltpu.SemaphoreType.DMA((1 + NX,)),
        ],
        compiler_params=pltpu.CompilerParams(
            collective_id=0, has_side_effects=True, vmem_limit_bytes=VMEM_LIMIT
        ),
        name="gather_adapters",
    )(slot_tab, *shards, base_weight.reshape(cut))
    return outs[:count], outs[count].reshape(members, depth, width)


def scatter_kernel(own, tab, tokens, weight, adapter, *refs):
    count = len(SCATTER_CHUNKS)
    key = refs[2 * count]
    refs = refs[: 2 * count] + refs[2 * count + 1 :]
    take = lambda i: refs[i * count : (i + 1) * count]
    grads, outs, lands, runs, sends1, lands1, sends2, lands2 = (take(i) for i in range(8))
    frozen, fs_send, fs_recv, s1_send, s1_recv, s2_send, s2_recv = refs[8 * count :]
    members = lax.axis_size("fsdp")
    blocks = grads[0].shape[0]
    cap = blocks // members
    pairs = NX * NZ * SLOTS
    sums = NX * NZ * own
    member = lax.axis_index("fsdp")
    group = lax.axis_index("dp")
    x, z = group // NZ, lax.rem(group, NZ)
    mesh_ids = pl.DeviceIdType.MESH
    at_x = lambda i: {"dp": dp_at(i, z)}
    at_z = lambda i: {"dp": dp_at(x, i)}

    barrier = pltpu.get_barrier_semaphore()
    for off in range(1, members):
        pl.semaphore_signal(
            barrier, inc=1, device_id={"fsdp": lax.rem(member + off, members)},
            device_id_type=mesh_ids,
        )
    for off in range(1, NX):
        pl.semaphore_signal(
            barrier, inc=1, device_id=at_x(lax.rem(x + off, NX)), device_id_type=mesh_ids
        )
    for off in range(1, NZ):
        pl.semaphore_signal(
            barrier, inc=1, device_id=at_z(lax.rem(z + off, NZ)), device_id_type=mesh_ids
        )
    pl.semaphore_wait(barrier, members - 1 + NX - 1 + NZ - 1)

    pending = []

    def exchange(src, dst, n, me, rows, target, send_sem, recv_sem, base):
        waits = []
        for off in range(1, n):
            peer = lax.rem(me + off, n)
            source = lax.rem(me - off + n, n)
            copy = pltpu.make_async_remote_copy(
                src_ref=src.at[pl.ds(peer * rows, rows)], dst_ref=dst.at[pl.ds(me * rows, rows)],
                send_sem=send_sem.at[base + off], recv_sem=recv_sem.at[base + off],
                device_id=target(peer), device_id_type=mesh_ids,
            )
            copy.start()
            pending.append(copy)
            waits.append(
                pltpu.make_async_remote_copy(
                    src_ref=src.at[pl.ds(source * rows, rows)],
                    dst_ref=dst.at[pl.ds(source * rows, rows)],
                    send_sem=send_sem.at[base + off], recv_sem=recv_sem.at[base + off],
                    device_id=target(source), device_id_type=mesh_ids,
                ).wait_recv
            )
        dst[pl.ds(me * rows, rows)] = src[pl.ds(me * rows, rows)]
        return waits

    fs_waits = [
        exchange(
            grads[c], lands[c], members, member, cap, lambda i: {"fsdp": i}, fs_send, fs_recv,
            c * members,
        )
        for c in range(count)
    ]
    depth = weight.shape[1]
    frozen[...] = adapter[...]

    def multiply(k, carry):
        columns = pl.ds(pl.multiple_of(k * depth, depth), depth)
        frozen[...] += jnp.dot(tokens[:, columns], weight[k], preferred_element_type=jnp.float32)
        return carry

    lax.fori_loop(0, weight.shape[0], multiply, 0)
    place = lax.broadcasted_iota(jnp.int32, frozen.shape, 0) // (frozen.shape[0] // cap)
    live = tab[blocks + 2 * pairs + 2 * sums]
    key[...] = jnp.where(place < live, frozen[...], 0.0).astype(key.dtype)

    waits1, waits2 = [], []

    def first_stage(c, order):
        n1, first = (NX, x) if order[0] == "x" else (NZ, z)
        target = at_x if order[0] == "x" else at_z
        kind = blocks + (0 if order[0] == "x" else pairs)
        run, send, land1 = runs[c], sends1[c], lands1[c]
        run[pl.ds(blocks, 1)] = jnp.zeros((1,) + run.shape[1:], run.dtype)
        land1[pl.ds(pairs, 1)] = jnp.zeros((1,) + land1.shape[1:], land1.dtype)
        for wait in fs_waits[c]:
            wait()

        def add(b, carry, run=run, land=lands[c]):
            run[pl.ds(b, 1)] = land[pl.ds(b, 1)].astype(jnp.float32) + run[pl.ds(tab[b], 1)]
            return carry

        lax.fori_loop(0, blocks, add, 0)

        def pick(p, carry, run=run, send=send, kind=kind):
            send[pl.ds(p, 1)] = run[pl.ds(tab[kind + p], 1)].astype(jnp.bfloat16)
            return carry

        lax.fori_loop(0, pairs, pick, 0)
        waits1.append(
            exchange(send, land1, n1, first, pairs // n1, target, s1_send, s1_recv, c * NZ)
        )

    def second_stage(c, order):
        n1, n2, second = (NX, NZ, z) if order[0] == "x" else (NZ, NX, x)
        target = at_z if order[0] == "x" else at_x
        kind = blocks + 2 * pairs + (0 if order[0] == "x" else sums)
        for wait in waits1[c]:
            wait()

        def total(q, carry, n1=n1, n2=n2, kind=kind, land1=lands1[c], send2=sends2[c]):
            acc = land1[pl.ds(tab[kind + q], 1)].astype(jnp.float32)
            for f in range(1, n1):
                acc = acc + land1[pl.ds(tab[kind + f * (n2 * own) + q], 1)].astype(jnp.float32)
            send2[pl.ds(q, 1)] = acc.astype(jnp.bfloat16)
            return carry

        lax.fori_loop(0, n2 * own, total, 0)
        waits2.append(
            exchange(sends2[c], lands2[c], n2, second, own, target, s2_send, s2_recv, c * NZ)
        )

    for c, (_, order) in enumerate(SCATTER_CHUNKS):
        first_stage(c, order)
        if c > 0:
            second_stage(c - 1, SCATTER_CHUNKS[c - 1][1])
    second_stage(count - 1, SCATTER_CHUNKS[-1][1])
    for c, (_, order) in enumerate(SCATTER_CHUNKS):
        n2 = NZ if order[0] == "x" else NX
        for wait in waits2[c]:
            wait()
        for j in range(own):
            acc = lands2[c][j].astype(jnp.float32)
            for s in range(1, n2):
                acc = acc + lands2[c][s * own + j].astype(jnp.float32)
            outs[c][j] = acc
    for copy in pending:
        copy.wait_send()


def scatter_gradients(packed, tab, tokens, full_weight, adapter, own, members):
    count = len(SCATTER_CHUNKS)
    blocks = packed.shape[0]
    pairs = NX * NZ * SLOTS
    grads, start = [], 0
    for rows, _ in SCATTER_CHUNKS:
        grads.append(packed[:, start : start + rows])
        start += rows
    vmem = pl.BlockSpec(memory_space=pltpu.VMEM)
    bf, f32 = jnp.bfloat16, jnp.float32
    second = [(NZ if order[0] == "x" else NX) * own for _, order in SCATTER_CHUNKS]
    buffers = lambda sizes, kind: [
        pltpu.VMEM((size, rows, LANES), kind) for size, (rows, _) in zip(sizes, SCATTER_CHUNKS)
    ]
    outs = pl.pallas_call(
        functools.partial(scatter_kernel, own),
        out_shape=[jax.ShapeDtypeStruct((own, rows, LANES), f32) for rows, _ in SCATTER_CHUNKS]
        + [jax.ShapeDtypeStruct(adapter.shape, bf)],
        in_specs=[pl.BlockSpec(memory_space=pltpu.SMEM)] + [vmem] * (count + 3),
        out_specs=[vmem] * (count + 1),
        scratch_shapes=buffers([blocks] * count, bf)
        + buffers([blocks + 1] * count, f32)
        + buffers([pairs] * count, bf)
        + buffers([pairs + 1] * count, bf)
        + buffers(second, bf)
        + buffers(second, bf)
        + [pltpu.VMEM(adapter.shape, f32)]
        + [pltpu.SemaphoreType.DMA((count * members,))] * 2
        + [pltpu.SemaphoreType.DMA((count * NZ,))] * 4,
        compiler_params=pltpu.CompilerParams(
            collective_id=1, has_side_effects=True, vmem_limit_bytes=VMEM_LIMIT
        ),
        name="scatter_gradients",
    )(tab, tokens, full_weight, adapter, *grads)
    return jnp.concatenate(outs[:count], axis=1), outs[count]


def lane_rows(array):
    lead, (rows, width) = array.shape[:-2], array.shape[-2:]
    parts = array.reshape(lead + (rows, width // LANES, LANES))
    return jnp.swapaxes(parts, -3, -2).reshape(lead + (rows * width // LANES, LANES))


def from_lane_rows(array, rows):
    lead, count = array.shape[:-2], array.shape[-2] // rows
    parts = array.reshape(lead + (count, rows, LANES))
    return jnp.swapaxes(parts, -3, -2).reshape(lead + (rows, count * LANES))


def pack(down, up):
    parts = jnp.concatenate([lane_rows(down), lane_rows(up)], axis=-2)
    room = PIECE - parts.shape[-2]
    return jnp.pad(parts, [(0, 0)] * (parts.ndim - 2) + [(0, room), (0, 0)])


def local(
    tokens,
    base_weight,
    cotangent,
    tenant_of_block,
    slot_of_tenant,
    live_blocks,
    down_param,
    down_mom,
    down_var,
    up_param,
    up_mom,
    up_var,
):
    groups = lax.axis_size("dp")
    members = lax.axis_size("fsdp")
    own_count = down_param.shape[0]
    tenants = own_count * groups
    seg_total = tenant_of_block.shape[0]
    segment_capacity = seg_total // (groups * members)
    block_row_count = tokens.shape[0] // segment_capacity
    feat_width = tokens.shape[1]
    heads_weight = base_weight.shape[1]
    rank_sh = down_param.shape[1]
    me_group = lax.axis_index("dp")
    me_member = lax.axis_index("fsdp")
    highest = lax.Precision.HIGHEST
    tenant_range = jnp.arange(tenants, dtype=jnp.int32)
    block_slot = jnp.sum(
        jnp.where(tenant_of_block[:, None] == tenant_range[None, :], slot_of_tenant[None, :], 0),
        axis=1,
    )
    block_group = jnp.arange(seg_total, dtype=jnp.int32) // segment_capacity % groups
    slot_onehot = (block_slot[:, None] == tenant_range[None, :]).astype(jnp.float32)
    group_onehot = (block_group[:, None] == jnp.arange(groups, dtype=jnp.int32)[None, :]).astype(
        jnp.float32
    )
    need_count = jnp.dot(group_onehot.T, slot_onehot, precision=highest)
    need_int = (need_count > 0.5).astype(jnp.int32).reshape(groups, groups, own_count)
    rank_tab = jnp.cumsum(need_int, axis=2) - need_int
    rank_rows = jnp.dot(
        group_onehot, rank_tab.reshape(groups, tenants).astype(jnp.float32), precision=highest
    )
    block_rank = jnp.sum(rank_rows * slot_onehot, axis=1).astype(jnp.int32)
    block_pos = block_slot // own_count * SLOTS + block_rank
    group_blocks = (
        jnp.arange(members, dtype=jnp.int32)[:, None] * groups + me_group
    ) * segment_capacity + jnp.arange(segment_capacity, dtype=jnp.int32)[None, :]
    pick_pos = jnp.take(block_pos, group_blocks, axis=0).reshape(-1)
    table_pick = jnp.take(block_slot, group_blocks, axis=0).reshape(-1)
    pick_xz = table_pick
    owner = table_pick // own_count
    pick_zx = (owner % NZ * NX + owner // NZ) * own_count + table_pick % own_count
    slot_tab = jnp.concatenate(
        [pick_xz if order == "zx" else pick_zx for _, order in GATHER_CHUNKS]
    )
    down_used = down_param.astype(jnp.bfloat16)
    up_used = up_param.astype(jnp.bfloat16)
    pieces, full_weight = gather_adapters(
        pack(down_used, up_used), base_weight, slot_tab, members, segment_capacity
    )
    pieces = jnp.concatenate(pieces, axis=1)
    down_rows = rank_sh * feat_width // LANES
    up_rows = rank_sh * heads_weight // LANES
    by_rank = lambda rows: jnp.swapaxes(
        from_lane_rows(rows, rank_sh).reshape(members, segment_capacity, rank_sh, -1), 0, 1
    ).reshape(segment_capacity, members * rank_sh, -1)
    block_down = by_rank(pieces[:, :down_rows])
    block_up = by_rank(pieces[:, down_rows : down_rows + up_rows])
    own_blocks = members * segment_capacity
    place = jnp.arange(own_blocks, dtype=jnp.int32)
    same = (pick_pos[:, None] == pick_pos[None, :]) & (place[None, :] < place[:, None])
    earlier = jnp.max(jnp.where(same, place[None, :], -1), axis=1)
    earlier = jnp.where(earlier < 0, own_blocks, earlier)
    pair_range = jnp.arange(groups * SLOTS, dtype=jnp.int32)
    final = jnp.max(jnp.where(pick_pos[None, :] == pair_range[:, None], place[None, :], -1), axis=1)
    final = jnp.where(final < 0, own_blocks, final)
    final_zx = jnp.swapaxes(final.reshape(NX, NZ, SLOTS), 0, 1).reshape(-1)
    rank_or = jnp.where(need_int == 1, rank_tab, -1).reshape(NX, NZ, NX, NZ, own_count)
    me_x, me_z = me_group // NZ, me_group % NZ
    to_x = jnp.take(jnp.take(rank_or, me_z, axis=1), me_x, axis=1)
    to_z = jnp.take(jnp.take(rank_or, me_x, axis=0), me_z, axis=2)

    def landed(ranks):
        first, second, _ = ranks.shape
        base = jnp.arange(first * second, dtype=jnp.int32).reshape(first, second, 1) * SLOTS
        return jnp.where(ranks >= 0, base + ranks, groups * SLOTS).reshape(-1)

    live_count = live_blocks[me_member * groups + me_group]
    sum_tab = jnp.concatenate(
        [earlier, final, final_zx, landed(to_x), landed(to_z), live_count[None]]
    )
    live_mask = (jnp.arange(segment_capacity, dtype=jnp.int32) < live_count)[:, None, None]
    blocks = tokens.reshape(segment_capacity, block_row_count, feat_width)
    hidden_state = jnp.einsum(
        "cbx,crx->cbr", blocks, block_down, preferred_element_type=jnp.float32
    ).astype(jnp.bfloat16)
    adapter_output = jnp.einsum(
        "cbr,crk->cbk", hidden_state, block_up, preferred_element_type=jnp.float32
    )
    adapter_rows = (adapter_scale * adapter_output).reshape(tokens.shape[0], heads_weight)
    cot_blocks = cotangent.reshape(segment_capacity, block_row_count, heads_weight)
    cotangent_active = jnp.where(live_mask, cot_blocks, jnp.zeros_like(cot_blocks))
    up_gradient = (
        adapter_scale
        * jnp.einsum(
            "cbr,cbk->crk", hidden_state, cotangent_active, preferred_element_type=jnp.float32
        )
    ).astype(jnp.bfloat16)
    hidden_gradient = (
        adapter_scale
        * jnp.einsum("cbk,crk->cbr", cotangent_active, block_up, preferred_element_type=jnp.float32)
    ).astype(jnp.bfloat16)
    grad_down = jnp.einsum(
        "cbr,cbx->crx", hidden_gradient, blocks, preferred_element_type=jnp.float32
    ).astype(jnp.bfloat16)
    by_member = lambda rows: jnp.swapaxes(
        rows.reshape(segment_capacity, members, rank_sh, -1), 0, 1
    ).reshape(own_blocks, rank_sh, -1)
    grad_rows = pack(by_member(grad_down), by_member(up_gradient))
    sum_rows, key_proj = scatter_gradients(
        grad_rows, sum_tab, tokens, full_weight, adapter_rows, own_count, members
    )
    sum_down = from_lane_rows(sum_rows[:, :down_rows], rank_sh)
    sum_up = from_lane_rows(sum_rows[:, down_rows : down_rows + up_rows], rank_sh)
    new_down, new_down_mom, new_down_var = adam_update(down_param, down_mom, down_var, sum_down)
    new_up, new_up_mom, new_up_var = adam_update(up_param, up_mom, up_var, sum_up)
    return (key_proj, new_down, new_down_mom, new_down_var, new_up, new_up_mom, new_up_var)


def solution(mesh):
    return jax.shard_map(
        local,
        mesh=mesh,
        in_specs=(
            P(("fsdp", "dp"), None),
            P("fsdp", None),
            P(("fsdp", "dp"), None),
            P(),
            P(),
            P(),
            P("dp", "fsdp", None),
            P("dp", "fsdp", None),
            P("dp", "fsdp", None),
            P("dp", "fsdp", None),
            P("dp", "fsdp", None),
            P("dp", "fsdp", None),
        ),
        out_specs=(
            P(("fsdp", "dp"), None),
            P("dp", "fsdp", None),
            P("dp", "fsdp", None),
            P("dp", "fsdp", None),
            P("dp", "fsdp", None),
            P("dp", "fsdp", None),
            P("dp", "fsdp", None),
        ),
        check_vma=False,
    )
```

```python
import functools

import jax
import jax.numpy as jnp
from jax import lax
from jax.experimental import pallas as pl
from jax.experimental.pallas import tpu as pltpu
from jax.sharding import PartitionSpec as P

SLOTS = 2
LANES = 128
NX, NZ = 4, 8
GATHER_CHUNKS = ((32, "zx"), (32, "xz"), (48, "zx"), (40, "xz"))
SCATTER_CHUNKS = ((32, "zx"), (48, "xz"), (40, "xz"), (32, "xz"))
FLOW_ORDER = (0, 1, 4) * 3 + (2, 3, 0, 1) * 3 + (2, 3, 4) + (3, 2) * 2 + (4, 4)
PIECE = 152
VMEM_LIMIT = 60 * 1024 * 1024


adapter_scale = 2.0
learn_rate = 0.01
beta_one = 0.9
beta_two = 0.99
adam_eps = 1e-08
correct_one = 1.0 - 0.9**8
correct_two = 1.0 - 0.99**8


def adam_update(master, moment, second, gradient):
    moment_new = beta_one * moment + (1.0 - beta_one) * gradient
    second_new = beta_two * second + (1.0 - beta_two) * gradient * gradient
    master_new = master - learn_rate * (moment_new / correct_one) / (
        jnp.sqrt(second_new / correct_two) + adam_eps
    )
    return (master_new, moment_new, second_new)


def dp_at(x, z):
    return x * NZ + z


def ring(send, n, me, unit, row_of, arrived=None):
    half = (unit + 1) // 2
    for step in range(1, n // 2 + 1):
        last = step == n // 2
        lo = (0, half if last else unit)
        hi = (half if last else 0, unit)
        out_r = row_of(lax.rem(me - (step - 1) + n, n))
        out_l = row_of(lax.rem(me + (step - 1), n))
        in_r = row_of(lax.rem(me - step + n, n))
        in_l = row_of(lax.rem(me + step, n))
        wait_r = send(+1, out_r + lo[0], lo[1] - lo[0], in_r + lo[0])
        wait_l = send(-1, out_l + hi[0], hi[1] - hi[0], in_l + hi[0])
        yield
        wait_r()
        wait_l()
        if arrived is not None:
            arrived(lax.rem(me - step + n, n), *lo)
            arrived(lax.rem(me + step, n), *hi)


def gather_kernel(own, slot_ref, *refs):
    count = len(GATHER_CHUNKS)
    shards, outs = refs[:count], refs[count + 1 : 2 * count + 1]
    weight_in, weight = refs[count], refs[2 * count + 1]
    refs = refs[2 * count + 2 :]
    tables, sends = refs[:count], refs[count : 2 * count]
    (
        send_sem, recv_sem, fs_send, fs_recv, ring_send, ring_recv, pair_send, pair_recv
    ) = refs[2 * count :]
    members = lax.axis_size("fsdp")
    blocks = sends[0].shape[0]
    cap = blocks // members
    member = lax.axis_index("fsdp")
    group = lax.axis_index("dp")
    x, z = group // NZ, lax.rem(group, NZ)
    chips = members // 2
    y, core = member // 2, lax.rem(member, 2)

    def shifted(axis, delta):
        if axis == "y":
            return {"fsdp": lax.rem(y + delta + chips, chips) * 2 + core}
        if axis == "x":
            return {"dp": dp_at(lax.rem(x + delta + NX, NX), z)}
        return {"dp": dp_at(x, lax.rem(z + delta + NZ, NZ))}

    barrier = pltpu.get_barrier_semaphore()
    for axis in ("x", "z"):
        for delta in (1, -1):
            pl.semaphore_signal(
                barrier, inc=1, device_id=shifted(axis, delta),
                device_id_type=pl.DeviceIdType.MESH,
            )
    for off in range(1, members):
        pl.semaphore_signal(
            barrier, inc=1, device_id={"fsdp": lax.rem(member + off, members)},
            device_id_type=pl.DeviceIdType.MESH,
        )
    for c, (_, order) in enumerate(GATHER_CHUNKS):
        minor_n = NZ if order == "zx" else NX
        major, minor = (x, z) if order == "zx" else (z, x)
        tables[c][pl.ds((major * minor_n + minor) * own, own)] = shards[c][...]
    weight[y, core, x] = weight_in[x]
    pl.semaphore_wait(barrier, 4 + members - 1)

    pending = []
    used = [0]

    def mover(table, axis):
        def send(delta, row, size, row_in):
            k = used[0]
            used[0] += 1
            dst = shifted(axis, delta)
            out = pltpu.make_async_remote_copy(
                src_ref=table.at[pl.ds(row, size)], dst_ref=table.at[pl.ds(row, size)],
                send_sem=send_sem.at[k], recv_sem=recv_sem.at[k],
                device_id=dst, device_id_type=pl.DeviceIdType.MESH,
            )
            out.start()
            pending.append(out)
            landed = pltpu.make_async_remote_copy(
                src_ref=table.at[pl.ds(row_in, size)], dst_ref=table.at[pl.ds(row_in, size)],
                send_sem=send_sem.at[k], recv_sem=recv_sem.at[k],
                device_id=dst, device_id_type=pl.DeviceIdType.MESH,
            )
            return landed.wait_recv

        return send

    def chunk_flow(c, order):
        table = tables[c]
        first, second = order
        n1, n2 = (NZ, NX) if order == "zx" else (NX, NZ)
        minor, major = (z, x) if order == "zx" else (x, z)
        yield from ring(
            mover(table, first), n1, minor, own, lambda i: (major * n1 + i) * own
        )
        yield from ring(mover(table, second), n2, major, n1 * own, lambda i: i * n1 * own)

        def pick(b, carry):
            sends[c][pl.ds(b, 1)] = table[pl.ds(slot_ref[c * blocks + b], 1)]
            return carry

        lax.fori_loop(0, blocks, pick, 0)
        outs[c][pl.ds(member * cap, cap)] = sends[c][pl.ds(member * cap, cap)]
        for off in range(1, members):
            peer = lax.rem(member + off, members)
            k = c * members + off
            out = pltpu.make_async_remote_copy(
                src_ref=sends[c].at[pl.ds(peer * cap, cap)],
                dst_ref=outs[c].at[pl.ds(member * cap, cap)],
                send_sem=fs_send.at[k], recv_sem=fs_recv.at[k],
                device_id={"fsdp": peer}, device_id_type=pl.DeviceIdType.MESH,
            )
            out.start()
            pending.append(out)

    ring_used = [0]
    pair_waits = []

    def weight_copy(here, there, dst, sems, k):
        copies = [
            pltpu.make_async_remote_copy(
                src_ref=at, dst_ref=at, send_sem=sems[0].at[k], recv_sem=sems[1].at[k],
                device_id=dst, device_id_type=pl.DeviceIdType.MESH,
            )
            for at in (here, there)
        ]
        copies[0].start()
        pending.append(copies[0])
        return copies[1].wait_recv

    def weight_mover(axis, part):
        def send(delta, row, size, row_in):
            k = ring_used[0]
            ring_used[0] += 1
            return weight_copy(
                part(row, size), part(row_in, size), shifted(axis, delta), (ring_send, ring_recv), k
            )

        return send

    def to_other_core(i, lo, hi):
        at = lambda which: weight.at[pl.ds(lo, hi - lo), which, i]
        pair_waits.append(
            weight_copy(
                at(core), at(1 - core), {"fsdp": y * 2 + 1 - core}, (pair_send, pair_recv),
                len(pair_waits),
            )
        )

    def weight_flow():
        along_y = lambda row, size: weight.at[row // 2, core, x, pl.ds(lax.rem(row, 2), size)]
        yield from ring(weight_mover("y", along_y), chips, y, 2, lambda i: i * 2)
        to_other_core(x, 0, chips)
        along_x = lambda row, size: weight.at[pl.ds(lax.rem(row, chips), size), core, row // chips]
        yield from ring(
            weight_mover("x", along_x), NX, x, chips, lambda i: i * chips, to_other_core
        )

    flows = [chunk_flow(c, order) for c, (_, order) in enumerate(GATHER_CHUNKS)]
    flows.append(weight_flow())
    for flow in flows:
        next(flow)
    for turn in FLOW_ORDER:
        next(flows[turn], None)
    for wait in pair_waits:
        wait()
    for c in range(count):
        for off in range(1, members):
            source = lax.rem(member - off + members, members)
            k = c * members + off
            pltpu.make_async_remote_copy(
                src_ref=sends[c].at[pl.ds(source * cap, cap)],
                dst_ref=outs[c].at[pl.ds(source * cap, cap)],
                send_sem=fs_send.at[k], recv_sem=fs_recv.at[k],
                device_id={"fsdp": source}, device_id_type=pl.DeviceIdType.MESH,
            ).wait_recv()
    for copy in pending:
        copy.wait_send()


def gather_adapters(packed, base_weight, slot_tab, members, cap):
    own = packed.shape[0]
    tenants = own * NX * NZ
    count = len(GATHER_CHUNKS)
    blocks = members * cap
    shards, start = [], 0
    for rows, _ in GATHER_CHUNKS:
        shards.append(packed[:, start : start + rows])
        start += rows
    vmem = pl.BlockSpec(memory_space=pltpu.VMEM)
    moves = count * 2 * (NX // 2 + NZ // 2)
    depth, width = base_weight.shape
    cut = (NX, 2, depth // NX // 2, width)
    outs = pl.pallas_call(
        functools.partial(gather_kernel, own),
        out_shape=[
            jax.ShapeDtypeStruct((blocks, rows, LANES), jnp.bfloat16) for rows, _ in GATHER_CHUNKS
        ]
        + [jax.ShapeDtypeStruct((members // 2, 2) + cut, jnp.bfloat16)],
        in_specs=[pl.BlockSpec(memory_space=pltpu.SMEM)] + [vmem] * (count + 1),
        out_specs=[vmem] * (count + 1),
        scratch_shapes=[pltpu.VMEM((tenants, rows, LANES), jnp.bfloat16) for rows, _ in GATHER_CHUNKS]
        + [pltpu.VMEM((blocks, rows, LANES), jnp.bfloat16) for rows, _ in GATHER_CHUNKS]
        + [
            pltpu.SemaphoreType.DMA((moves,)),
            pltpu.SemaphoreType.DMA((moves,)),
            pltpu.SemaphoreType.DMA((count * members,)),
            pltpu.SemaphoreType.DMA((count * members,)),
            pltpu.SemaphoreType.DMA((members // 2 + NX,)),
            pltpu.SemaphoreType.DMA((members // 2 + NX,)),
            pltpu.SemaphoreType.DMA((1 + NX,)),
            pltpu.SemaphoreType.DMA((1 + NX,)),
        ],
        compiler_params=pltpu.CompilerParams(
            collective_id=0, has_side_effects=True, vmem_limit_bytes=VMEM_LIMIT
        ),
        name="gather_adapters",
    )(slot_tab, *shards, base_weight.reshape(cut))
    return outs[:count], outs[count].reshape(members, depth, width)


def scatter_kernel(own, tab, tokens, weight, adapter, *refs):
    count = len(SCATTER_CHUNKS)
    key = refs[2 * count]
    refs = refs[: 2 * count] + refs[2 * count + 1 :]
    take = lambda i: refs[i * count : (i + 1) * count]
    grads, outs, lands, runs, sends1, lands1, sends2, lands2 = (take(i) for i in range(8))
    frozen, fs_send, fs_recv, s1_send, s1_recv, s2_send, s2_recv = refs[8 * count :]
    members = lax.axis_size("fsdp")
    blocks = grads[0].shape[0]
    cap = blocks // members
    pairs = NX * NZ * SLOTS
    sums = NX * NZ * own
    member = lax.axis_index("fsdp")
    group = lax.axis_index("dp")
    x, z = group // NZ, lax.rem(group, NZ)
    mesh_ids = pl.DeviceIdType.MESH
    at_x = lambda i: {"dp": dp_at(i, z)}
    at_z = lambda i: {"dp": dp_at(x, i)}

    barrier = pltpu.get_barrier_semaphore()
    for off in range(1, members):
        pl.semaphore_signal(
            barrier, inc=1, device_id={"fsdp": lax.rem(member + off, members)},
            device_id_type=mesh_ids,
        )
    for off in range(1, NX):
        pl.semaphore_signal(
            barrier, inc=1, device_id=at_x(lax.rem(x + off, NX)), device_id_type=mesh_ids
        )
    for off in range(1, NZ):
        pl.semaphore_signal(
            barrier, inc=1, device_id=at_z(lax.rem(z + off, NZ)), device_id_type=mesh_ids
        )
    pl.semaphore_wait(barrier, members - 1 + NX - 1 + NZ - 1)

    pending = []

    def exchange(src, dst, n, me, rows, target, send_sem, recv_sem, base):
        waits = []
        for off in range(1, n):
            peer = lax.rem(me + off, n)
            source = lax.rem(me - off + n, n)
            copy = pltpu.make_async_remote_copy(
                src_ref=src.at[pl.ds(peer * rows, rows)], dst_ref=dst.at[pl.ds(me * rows, rows)],
                send_sem=send_sem.at[base + off], recv_sem=recv_sem.at[base + off],
                device_id=target(peer), device_id_type=mesh_ids,
            )
            copy.start()
            pending.append(copy)
            waits.append(
                pltpu.make_async_remote_copy(
                    src_ref=src.at[pl.ds(source * rows, rows)],
                    dst_ref=dst.at[pl.ds(source * rows, rows)],
                    send_sem=send_sem.at[base + off], recv_sem=recv_sem.at[base + off],
                    device_id=target(source), device_id_type=mesh_ids,
                ).wait_recv
            )
        dst[pl.ds(me * rows, rows)] = src[pl.ds(me * rows, rows)]
        return waits

    fs_waits = [
        exchange(
            grads[c], lands[c], members, member, cap, lambda i: {"fsdp": i}, fs_send, fs_recv,
            c * members,
        )
        for c in range(count)
    ]
    depth = weight.shape[1]
    frozen[...] = adapter[...]

    def multiply(k, carry):
        columns = pl.ds(pl.multiple_of(k * depth, depth), depth)
        frozen[...] += jnp.dot(tokens[:, columns], weight[k], preferred_element_type=jnp.float32)
        return carry

    lax.fori_loop(0, weight.shape[0], multiply, 0)
    place = lax.broadcasted_iota(jnp.int32, frozen.shape, 0) // (frozen.shape[0] // cap)
    live = tab[blocks + 2 * pairs + 2 * sums]
    key[...] = jnp.where(place < live, frozen[...], 0.0).astype(key.dtype)

    waits1, waits2 = [], []

    def first_stage(c, order):
        n1, first = (NX, x) if order[0] == "x" else (NZ, z)
        target = at_x if order[0] == "x" else at_z
        kind = blocks + (0 if order[0] == "x" else pairs)
        run, send, land1 = runs[c], sends1[c], lands1[c]
        run[pl.ds(blocks, 1)] = jnp.zeros((1,) + run.shape[1:], run.dtype)
        land1[pl.ds(pairs, 1)] = jnp.zeros((1,) + land1.shape[1:], land1.dtype)
        for wait in fs_waits[c]:
            wait()

        def add(b, carry, run=run, land=lands[c]):
            run[pl.ds(b, 1)] = land[pl.ds(b, 1)].astype(jnp.float32) + run[pl.ds(tab[b], 1)]
            return carry

        lax.fori_loop(0, blocks, add, 0)

        def pick(p, carry, run=run, send=send, kind=kind):
            send[pl.ds(p, 1)] = run[pl.ds(tab[kind + p], 1)].astype(jnp.bfloat16)
            return carry

        lax.fori_loop(0, pairs, pick, 0)
        waits1.append(
            exchange(send, land1, n1, first, pairs // n1, target, s1_send, s1_recv, c * NZ)
        )

    def second_stage(c, order):
        n1, n2, second = (NX, NZ, z) if order[0] == "x" else (NZ, NX, x)
        target = at_z if order[0] == "x" else at_x
        kind = blocks + 2 * pairs + (0 if order[0] == "x" else sums)
        for wait in waits1[c]:
            wait()

        def total(q, carry, n1=n1, n2=n2, kind=kind, land1=lands1[c], send2=sends2[c]):
            acc = land1[pl.ds(tab[kind + q], 1)].astype(jnp.float32)
            for f in range(1, n1):
                acc = acc + land1[pl.ds(tab[kind + f * (n2 * own) + q], 1)].astype(jnp.float32)
            send2[pl.ds(q, 1)] = acc.astype(jnp.bfloat16)
            return carry

        lax.fori_loop(0, n2 * own, total, 0)
        waits2.append(
            exchange(sends2[c], lands2[c], n2, second, own, target, s2_send, s2_recv, c * NZ)
        )

    for c, (_, order) in enumerate(SCATTER_CHUNKS):
        first_stage(c, order)
        if c > 0:
            second_stage(c - 1, SCATTER_CHUNKS[c - 1][1])
    second_stage(count - 1, SCATTER_CHUNKS[-1][1])
    for c, (_, order) in enumerate(SCATTER_CHUNKS):
        n2 = NZ if order[0] == "x" else NX
        for wait in waits2[c]:
            wait()
        for j in range(own):
            acc = lands2[c][j].astype(jnp.float32)
            for s in range(1, n2):
                acc = acc + lands2[c][s * own + j].astype(jnp.float32)
            outs[c][j] = acc
    for copy in pending:
        copy.wait_send()


def scatter_gradients(packed, tab, tokens, full_weight, adapter, own, members):
    count = len(SCATTER_CHUNKS)
    blocks = packed.shape[0]
    pairs = NX * NZ * SLOTS
    grads, start = [], 0
    for rows, _ in SCATTER_CHUNKS:
        grads.append(packed[:, start : start + rows])
        start += rows
    vmem = pl.BlockSpec(memory_space=pltpu.VMEM)
    bf, f32 = jnp.bfloat16, jnp.float32
    second = [(NZ if order[0] == "x" else NX) * own for _, order in SCATTER_CHUNKS]
    buffers = lambda sizes, kind: [
        pltpu.VMEM((size, rows, LANES), kind) for size, (rows, _) in zip(sizes, SCATTER_CHUNKS)
    ]
    outs = pl.pallas_call(
        functools.partial(scatter_kernel, own),
        out_shape=[jax.ShapeDtypeStruct((own, rows, LANES), f32) for rows, _ in SCATTER_CHUNKS]
        + [jax.ShapeDtypeStruct(adapter.shape, bf)],
        in_specs=[pl.BlockSpec(memory_space=pltpu.SMEM)] + [vmem] * (count + 3),
        out_specs=[vmem] * (count + 1),
        scratch_shapes=buffers([blocks] * count, bf)
        + buffers([blocks + 1] * count, f32)
        + buffers([pairs] * count, bf)
        + buffers([pairs + 1] * count, bf)
        + buffers(second, bf)
        + buffers(second, bf)
        + [pltpu.VMEM(adapter.shape, f32)]
        + [pltpu.SemaphoreType.DMA((count * members,))] * 2
        + [pltpu.SemaphoreType.DMA((count * NZ,))] * 4,
        compiler_params=pltpu.CompilerParams(
            collective_id=1, has_side_effects=True, vmem_limit_bytes=VMEM_LIMIT
        ),
        name="scatter_gradients",
    )(tab, tokens, full_weight, adapter, *grads)
    return jnp.concatenate(outs[:count], axis=1), outs[count]


def lane_rows(array):
    lead, (rows, width) = array.shape[:-2], array.shape[-2:]
    parts = array.reshape(lead + (rows, width // LANES, LANES))
    return jnp.swapaxes(parts, -3, -2).reshape(lead + (rows * width // LANES, LANES))


def from_lane_rows(array, rows):
    lead, count = array.shape[:-2], array.shape[-2] // rows
    parts = array.reshape(lead + (count, rows, LANES))
    return jnp.swapaxes(parts, -3, -2).reshape(lead + (rows, count * LANES))


def pack(down, up):
    parts = jnp.concatenate([lane_rows(down), lane_rows(up)], axis=-2)
    room = PIECE - parts.shape[-2]
    return jnp.pad(parts, [(0, 0)] * (parts.ndim - 2) + [(0, room), (0, 0)])


def local(
    tokens,
    base_weight,
    cotangent,
    tenant_of_block,
    slot_of_tenant,
    live_blocks,
    down_param,
    down_mom,
    down_var,
    up_param,
    up_mom,
    up_var,
):
    groups = lax.axis_size("dp")
    members = lax.axis_size("fsdp")
    own_count = down_param.shape[0]
    tenants = own_count * groups
    seg_total = tenant_of_block.shape[0]
    segment_capacity = seg_total // (groups * members)
    block_row_count = tokens.shape[0] // segment_capacity
    feat_width = tokens.shape[1]
    heads_weight = base_weight.shape[1]
    rank_sh = down_param.shape[1]
    me_group = lax.axis_index("dp")
    me_member = lax.axis_index("fsdp")
    highest = lax.Precision.HIGHEST
    tenant_range = jnp.arange(tenants, dtype=jnp.int32)
    block_slot = jnp.sum(
        jnp.where(tenant_of_block[:, None] == tenant_range[None, :], slot_of_tenant[None, :], 0),
        axis=1,
    )
    block_group = jnp.arange(seg_total, dtype=jnp.int32) // segment_capacity % groups
    slot_onehot = (block_slot[:, None] == tenant_range[None, :]).astype(jnp.float32)
    group_onehot = (block_group[:, None] == jnp.arange(groups, dtype=jnp.int32)[None, :]).astype(
        jnp.float32
    )
    need_count = jnp.dot(group_onehot.T, slot_onehot, precision=highest)
    need_int = (need_count > 0.5).astype(jnp.int32).reshape(groups, groups, own_count)
    rank_tab = jnp.cumsum(need_int, axis=2) - need_int
    rank_rows = jnp.dot(
        group_onehot, rank_tab.reshape(groups, tenants).astype(jnp.float32), precision=highest
    )
    block_rank = jnp.sum(rank_rows * slot_onehot, axis=1).astype(jnp.int32)
    block_pos = block_slot // own_count * SLOTS + block_rank
    group_blocks = (
        jnp.arange(members, dtype=jnp.int32)[:, None] * groups + me_group
    ) * segment_capacity + jnp.arange(segment_capacity, dtype=jnp.int32)[None, :]
    pick_pos = jnp.take(block_pos, group_blocks, axis=0).reshape(-1)
    table_pick = jnp.take(block_slot, group_blocks, axis=0).reshape(-1)
    pick_xz = table_pick
    owner = table_pick // own_count
    pick_zx = (owner % NZ * NX + owner // NZ) * own_count + table_pick % own_count
    slot_tab = jnp.concatenate(
        [pick_xz if order == "zx" else pick_zx for _, order in GATHER_CHUNKS]
    )
    down_used = down_param.astype(jnp.bfloat16)
    up_used = up_param.astype(jnp.bfloat16)
    pieces, full_weight = gather_adapters(
        pack(down_used, up_used), base_weight, slot_tab, members, segment_capacity
    )
    pieces = jnp.concatenate(pieces, axis=1)
    down_rows = rank_sh * feat_width // LANES
    up_rows = rank_sh * heads_weight // LANES
    by_rank = lambda rows: jnp.swapaxes(
        from_lane_rows(rows, rank_sh).reshape(members, segment_capacity, rank_sh, -1), 0, 1
    ).reshape(segment_capacity, members * rank_sh, -1)
    block_down = by_rank(pieces[:, :down_rows])
    block_up = by_rank(pieces[:, down_rows : down_rows + up_rows])
    own_blocks = members * segment_capacity
    place = jnp.arange(own_blocks, dtype=jnp.int32)
    same = (pick_pos[:, None] == pick_pos[None, :]) & (place[None, :] < place[:, None])
    earlier = jnp.max(jnp.where(same, place[None, :], -1), axis=1)
    earlier = jnp.where(earlier < 0, own_blocks, earlier)
    pair_range = jnp.arange(groups * SLOTS, dtype=jnp.int32)
    final = jnp.max(jnp.where(pick_pos[None, :] == pair_range[:, None], place[None, :], -1), axis=1)
    final = jnp.where(final < 0, own_blocks, final)
    final_zx = jnp.swapaxes(final.reshape(NX, NZ, SLOTS), 0, 1).reshape(-1)
    rank_or = jnp.where(need_int == 1, rank_tab, -1).reshape(NX, NZ, NX, NZ, own_count)
    me_x, me_z = me_group // NZ, me_group % NZ
    to_x = jnp.take(jnp.take(rank_or, me_z, axis=1), me_x, axis=1)
    to_z = jnp.take(jnp.take(rank_or, me_x, axis=0), me_z, axis=2)

    def landed(ranks):
        first, second, _ = ranks.shape
        base = jnp.arange(first * second, dtype=jnp.int32).reshape(first, second, 1) * SLOTS
        return jnp.where(ranks >= 0, base + ranks, groups * SLOTS).reshape(-1)

    live_count = live_blocks[me_member * groups + me_group]
    sum_tab = jnp.concatenate(
        [earlier, final, final_zx, landed(to_x), landed(to_z), live_count[None]]
    )
    live_mask = (jnp.arange(segment_capacity, dtype=jnp.int32) < live_count)[:, None, None]
    blocks = tokens.reshape(segment_capacity, block_row_count, feat_width)
    hidden_state = jnp.einsum(
        "cbx,crx->cbr", blocks, block_down, preferred_element_type=jnp.float32
    ).astype(jnp.bfloat16)
    adapter_output = jnp.einsum(
        "cbr,crk->cbk", hidden_state, block_up, preferred_element_type=jnp.float32
    )
    adapter_rows = (adapter_scale * adapter_output).reshape(tokens.shape[0], heads_weight)
    cot_blocks = cotangent.reshape(segment_capacity, block_row_count, heads_weight)
    cotangent_active = jnp.where(live_mask, cot_blocks, jnp.zeros_like(cot_blocks))
    up_gradient = (
        adapter_scale
        * jnp.einsum(
            "cbr,cbk->crk", hidden_state, cotangent_active, preferred_element_type=jnp.float32
        )
    ).astype(jnp.bfloat16)
    hidden_gradient = (
        adapter_scale
        * jnp.einsum("cbk,crk->cbr", cotangent_active, block_up, preferred_element_type=jnp.float32)
    ).astype(jnp.bfloat16)
    grad_down = jnp.einsum(
        "cbr,cbx->crx", hidden_gradient, blocks, preferred_element_type=jnp.float32
    ).astype(jnp.bfloat16)
    by_member = lambda rows: jnp.swapaxes(
        rows.reshape(segment_capacity, members, rank_sh, -1), 0, 1
    ).reshape(own_blocks, rank_sh, -1)
    grad_rows = pack(by_member(grad_down), by_member(up_gradient))
    sum_rows, key_proj = scatter_gradients(
        grad_rows, sum_tab, tokens, full_weight, adapter_rows, own_count, members
    )
    sum_down = from_lane_rows(sum_rows[:, :down_rows], rank_sh)
    sum_up = from_lane_rows(sum_rows[:, down_rows : down_rows + up_rows], rank_sh)
    new_down, new_down_mom, new_down_var = adam_update(down_param, down_mom, down_var, sum_down)
    new_up, new_up_mom, new_up_var = adam_update(up_param, up_mom, up_var, sum_up)
    return (key_proj, new_down, new_down_mom, new_down_var, new_up, new_up_mom, new_up_var)


def solution(mesh):
    return jax.shard_map(
        local,
        mesh=mesh,
        in_specs=(
            P(("fsdp", "dp"), None),
            P("fsdp", None),
            P(("fsdp", "dp"), None),
            P(),
            P(),
            P(),
            P("dp", "fsdp", None),
            P("dp", "fsdp", None),
            P("dp", "fsdp", None),
            P("dp", "fsdp", None),
            P("dp", "fsdp", None),
            P("dp", "fsdp", None),
        ),
        out_specs=(
            P(("fsdp", "dp"), None),
            P("dp", "fsdp", None),
            P("dp", "fsdp", None),
            P("dp", "fsdp", None),
            P("dp", "fsdp", None),
            P("dp", "fsdp", None),
            P("dp", "fsdp", None),
        ),
        check_vma=False,
    )
```
